32 devices in a mesh: cand: 4 (over y, x), hist: 8 (over z, core).
Axes of the slice: x: 2, y: 2, z: 4, core: 2. Of those that a mesh axis runs over, the one named last changes fastest.
Arguments:
- inputs: bfloat16 [4, 256, 1024], P('cand', 'hist'), may hold values from -6 to 6
- in_gain: float32 [1024], replicated, may hold values from 0.1 to 1.9
- w_qu: bfloat16 [2, 1024, 1024], P(None, 'cand', 'hist'), may hold values from -0.1875 to 0.1875
- out_gain: float32 [1024], replicated, may hold values from 0.1 to 1.9
- w_out: bfloat16 [1024, 1024], P('hist', 'cand'), may hold values from -0.1875 to 0.1875
- hist_keys: bfloat16 [4, 4096, 1024], P('cand', 'hist'), may hold values from -6 to 6
- hist_values: bfloat16 [4, 4096, 1024], P('cand', 'hist'), may hold values from -6 to 6
- pos_bias: float32 [16, 16], replicated, may hold values from -4 to 4
- lengths: int32 [4], P('cand'), may hold values from 1 to 4096, 8192 in all
- tile_order: int32 [4, 16], P('cand', 'hist'), may hold values from 0 to 15, each once within a row
- tile_mask: int32 [4, 16], P('cand', 'hist'), may hold values 0 or 1
Outputs:
- scored: bfloat16 [4, 256, 1024], P('cand', 'hist')
The draws below stay inside these ranges and needn't reach their ends.
Inputs may be any that keep to these rules, and one draw needn't show every extreme that they name: `tile_order`: for each user, every logical tile number appears in exactly one of its 16 slots.
All inputs are finite; a program needn't handle non-finite values. No bound on the sum of `lengths` or of `tile_mask` on one device may be relied on, other than what follows from the above.
Results may differ from the reference program's by a relative error of at most 0.015.
Values may be sent and summed in bfloat16 or wider, within the bound.
A program may use at most 64 MiB of HBM per device.

```python
import math
import jax
import jax.numpy as jnp
import numpy as np
from jax import lax

D = 1024
HEADS = 16
TILE = 256
TILES_DEV = 2
CANDS_USER = 256
USERS = 4
TILES = 16
EVENTS = 4096
N_HIST = 8


def set_ends(drawn, own_key, low, top_value):
    longest = drawn.shape.index(max(drawn.shape))
    spots = []
    for shift in (0, 1):
        where = [jax.random.randint(jax.random.fold_in(own_key, axis), (), 0, length) for axis, length in enumerate(drawn.shape)]
        where[longest] = (where[longest] + shift) % drawn.shape[longest]
        spots.append(tuple(where))
    return drawn.at[spots[0]].set(low).at[spots[1]].set(top_value)


def level_of(key, dims, pieces, least, high):
    level, own = 1.0, jax.random.fold_in(key, 6)
    for position, shards_of in pieces:
        steps = jnp.exp(jax.random.uniform(jax.random.fold_in(own, position), (shards_of,), jnp.float32, least / len(pieces), high / len(pieces)))
        level = level * jnp.repeat(steps, dims[position] // shards_of).reshape([-1 if axis == position else 1 for axis in range(len(dims))])
    return level


def length_profile(count, total, reach, slope):
    weights = [(1 << 20) // math.isqrt(grade ** slope) + 1 for grade in range(2, count + 1)]
    surplus, given = total - reach - (count - 1), [1] * (count - 1)
    while surplus > 0:
        movable = [i for i in range(count - 1) if given[i] < reach]
        whole, remaining = sum([weights[i] for i in movable]), surplus
        for i in movable:
            addition = min(reach - given[i], max(1, remaining * weights[i] // whole), surplus)
            given[i] = given[i] + addition
            surplus = surplus - addition
    return np.array([reach] + given)


def ragged_sizes(stream_key, count, total, most, lean):
    if count == 2:
        one = jax.random.randint(stream_key, (), max(1, total - most), min(most, total - 1) + 1)
        return jnp.stack([one, total - one])
    tallies = jnp.asarray(length_profile(count, total, most, lean), jnp.int32)
    twos = (count - 1) // 2
    source_of, receiver = tallies[1:1 + 2 * twos:2], tallies[2:2 + 2 * twos:2]
    slack = jnp.minimum(source_of - 1, most - receiver)
    shifted = jax.random.randint(jax.random.fold_in(stream_key, 1), (twos,), 0, 1 << 20) % (slack + 1)
    tallies = tallies.at[1:1 + 2 * twos:2].set(source_of - shifted).at[2:2 + 2 * twos:2].set(receiver + shifted)
    return tallies[jax.random.permutation(jax.random.fold_in(stream_key, 2), count)]


def noise(rng, extent, spread, limit, pieces=(), kind=jnp.bfloat16):
    gain = level_of(rng, extent, pieces, -0.22, 0.18) if pieces else 1.0
    result = jax.random.normal(rng, extent, jnp.float32) * spread * gain
    return jnp.minimum(jnp.maximum(result, -limit), limit).astype(kind)


def setup_inputs(seed: int = 0) -> dict:
    keys = jax.random.split(jax.random.key(seed), 12)
    inputs = noise(keys[0], (USERS, CANDS_USER, D), 1.0, 6.0, ((0, 4), (1, 8)))
    in_gain = jnp.clip(1.0 + 0.18 * jax.random.normal(keys[1], (D,), jnp.float32), 0.1, 1.9)
    w_qu = noise(keys[2], (2, D, D), D ** -0.5, 0.1875, ((1, 4), (2, 8)))
    out_gain = jnp.clip(1.0 + 0.18 * jax.random.normal(keys[3], (D,), jnp.float32), 0.1, 1.9)
    w_out = noise(keys[4], (D, D), D ** -0.5, 0.1875, ((0, 8), (1, 4)))
    hist_keys = noise(keys[5], (USERS, EVENTS, D), 1.0, 6.0, ((0, 4), (1, 8)))
    hist_values = noise(keys[6], (USERS, EVENTS, D), 1.0, 6.0, ((0, 4), (1, 8)))
    pos_bias = noise(keys[7], (HEADS, TILES), 1.0, 4.0, (), jnp.float32)
    lengths = ragged_sizes(keys[8], USERS, USERS * EVENTS // 2, EVENTS, 2).astype(jnp.int32)
    tile_order = jax.vmap(lambda own: jax.random.permutation(own, TILES))(jax.random.split(keys[9], USERS)).reshape((USERS, TILES)).astype(jnp.int32)
    tile_mask = set_ends((jax.random.randint(keys[10], (USERS, TILES), 0, 4) < 3).astype(jnp.int32), jax.random.fold_in(keys[10], 1), 0, 1)
    return {"inputs": inputs, "in_gain": in_gain, "w_qu": w_qu, "out_gain": out_gain, "w_out": w_out, "hist_keys": hist_keys, "hist_values": hist_values, "pos_bias": pos_bias, "lengths": lengths, "tile_order": tile_order, "tile_mask": tile_mask}


EPS = 1e-05

def layer_norm(values, gain_vector):
    row_mean = lax.optimization_barrier(jnp.mean(values, axis=-1, keepdims=True))
    square = lax.optimization_barrier(jnp.mean(values * values, axis=-1, keepdims=True))
    return (values - row_mean) * lax.rsqrt(square - row_mean * row_mean + EPS) * gain_vector

def to_half(values):
    return lax.optimization_barrier(values.astype(jnp.bfloat16))

def reference(inputs, in_gain, w_qu, out_gain, w_out, hist_keys, hist_values, pos_bias, lengths, tile_order, tile_mask):
    normed = to_half(layer_norm(inputs.astype(jnp.float32), in_gain))
    projected = jnp.einsum('ucd,jde->ucje', normed.astype(jnp.float32), w_qu.astype(jnp.float32))
    queries = to_half(jax.nn.silu(projected[:, :, 0]))
    gates = jax.nn.silu(projected[:, :, 1])
    head_dim = D // HEADS
    score_scale = 1.0 / math.sqrt(head_dim)
    per_shard = TILES_DEV * TILE
    offsets = jnp.arange(per_shard, dtype=jnp.int32) % TILE

    def one_user(user_items):
        user_query, key_block, value_block, slot_order, slot_mask, length = user_items
        query_heads = user_query.astype(jnp.float32).reshape(CANDS_USER, HEADS, head_dim)
        key_block = key_block.reshape(N_HIST, per_shard, HEADS, head_dim)
        value_block = value_block.reshape(N_HIST, per_shard, HEADS, head_dim)
        slot_order = slot_order.reshape(N_HIST, TILES_DEV)
        slot_mask = slot_mask.reshape(N_HIST, TILES_DEV)

        def one_shard(summed, shard_items):
            shard_keys, shard_values, shard_order, shard_mask = shard_items
            event_order = jnp.repeat(shard_order, TILE)
            event_mask = jnp.repeat(shard_mask, TILE)
            is_live = ((event_mask == 1) & (event_order * TILE + offsets < length)).astype(jnp.float32)
            slot_bias = jnp.repeat(pos_bias[:, shard_order], TILE, axis=1)
            scores = jnp.einsum('chd,ehd->che', query_heads, shard_keys.astype(jnp.float32)) * score_scale + slot_bias[None]
            weights = to_half(jax.nn.silu(scores) * is_live[None, None, :])
            partial_value = jnp.einsum('che,ehd->chd', weights.astype(jnp.float32), shard_values.astype(jnp.float32))
            return (summed + partial_value.reshape(CANDS_USER, D), None)
        summed, _ = lax.scan(one_shard, jnp.zeros((CANDS_USER, D), jnp.float32), (key_block, value_block, slot_order, slot_mask))
        return summed
    attended = lax.map(one_user, (queries, hist_keys, hist_values, tile_order, tile_mask, lengths))
    gated = to_half(layer_norm(attended, out_gain) * gates)
    projected_out = jnp.dot(gated.reshape(-1, D), w_out, preferred_element_type=jnp.float32).reshape(inputs.shape)
    return (inputs.astype(jnp.float32) + projected_out).astype(jnp.bfloat16)
```

```python
import functools
import math

import jax
import jax.numpy as jnp
from jax import lax
from jax.experimental import pallas as pl
from jax.experimental.pallas import tpu as pltpu
from jax.sharding import PartitionSpec as P

EPS = 1e-05


def layer_norm(values, gain_vector):
    row_mean = jnp.mean(values, axis=-1, keepdims=True)
    square = jnp.mean(values * values, axis=-1, keepdims=True)
    return (values - row_mean) * lax.rsqrt(square - row_mean * row_mean + EPS) * gain_vector


def attention(all_queries, hist_keys, hist_values, pos_bias, lengths, tile_order, tile_mask):
    cands = all_queries.shape[1]
    width = all_queries.shape[2]
    heads = pos_bias.shape[0]
    tiles_all = pos_bias.shape[1]
    slots = tile_order.shape[1]
    tile = hist_keys.shape[1] // slots
    head_dim = width // heads
    score_scale = 1.0 / math.sqrt(head_dim)
    tile_numbers = jnp.arange(tiles_all, dtype=jnp.int32)
    offsets = jnp.arange(tile, dtype=jnp.int32)

    def one_user(user_items):
        user_query, key_block, value_block, slot_order, slot_mask, length = user_items
        query_heads = user_query.reshape(cands, heads, head_dim)
        one_hot = (slot_order[:, None] == tile_numbers[None, :]).astype(jnp.float32)
        slot_bias = jnp.dot(one_hot, pos_bias.T, precision=lax.Precision.HIGHEST)
        summed = jnp.zeros((cands, heads, head_dim), jnp.float32)
        for slot_index in range(slots):
            key_tile = key_block[slot_index * tile : (slot_index + 1) * tile].reshape(
                tile, heads, head_dim
            )
            value_tile = value_block[slot_index * tile : (slot_index + 1) * tile].reshape(
                tile, heads, head_dim
            )
            positions = slot_order[slot_index] * tile + offsets
            is_live = ((slot_mask[slot_index] == 1) & (positions < length)).astype(jnp.float32)
            bias_row = slot_bias[slot_index]

            def compute(
                key_tile=key_tile, value_tile=value_tile, is_live=is_live, bias_row=bias_row
            ):
                scores = jnp.einsum(
                    "chd,ehd->che", query_heads, key_tile, preferred_element_type=jnp.float32
                )
                scores = scores * score_scale + bias_row[None, :, None]
                weights = (jax.nn.silu(scores) * is_live[None, None, :]).astype(jnp.bfloat16)
                return jnp.einsum(
                    "che,ehd->chd", weights, value_tile, preferred_element_type=jnp.float32
                )

            summed = summed + compute()
        return summed.reshape(cands, width)

    return lax.map(one_user, (all_queries, hist_keys, hist_values, tile_order, tile_mask, lengths))


def shards(
    inputs,
    in_gain,
    w_qu,
    out_gain,
    w_out,
    hist_keys,
    hist_values,
    pos_bias,
    lengths,
    tile_order,
    tile_mask,
):
    w_full, out_rows = (
        lax.all_gather(w_qu, "cand", axis=1, tiled=True),
        lax.all_gather(w_out, "cand", axis=1, tiled=True),
    )
    normed = layer_norm(inputs.astype(jnp.float32), in_gain).astype(jnp.bfloat16)
    projected = jnp.einsum(
        "ucd,jdk->ucjk",
        normed,
        lax.all_gather(w_full, "hist", axis=2, tiled=True),
        preferred_element_type=jnp.float32,
    )
    queries = jax.nn.silu(projected[:, :, 0]).astype(jnp.bfloat16)
    gates = jax.nn.silu(projected[:, :, 1])
    all_queries = lax.all_gather(queries, "hist", axis=1, tiled=True)
    attended = attention(
        all_queries, hist_keys, hist_values, pos_bias, lengths, tile_order, tile_mask
    )
    own_rows = lax.psum_scatter(
        attended.astype(jnp.bfloat16), "hist", scatter_dimension=1, tiled=True
    ).astype(jnp.float32)
    gated = (layer_norm(own_rows, out_gain) * gates).astype(jnp.bfloat16)
    projected_out = jnp.einsum(
        "uck,kd->ucd",
        gated,
        lax.all_gather(out_rows, "hist", axis=0, tiled=True),
        preferred_element_type=jnp.float32,
    )
    return (inputs.astype(jnp.float32) + projected_out).astype(jnp.bfloat16)


MESH = pl.DeviceIdType.MESH
CORES = 2


def silu_of_half(half):
    return half + half * jnp.tanh(half)


def fused(
    n_cand, chips, inputs_hbm, in_gain_hbm, w_ref, out_gain_hbm, wo_ref, k_hbm, v_hbm, bias_hbm,
    len_hbm, order_hbm, mask_hbm, out_ref,
    inputs_ref, in_gain_ref, out_gain_ref, bias_ref, len_ref, order_ref, mask_ref, in_sem, xn,
    wq, wo, keys, vals, qs, gate_out, gate_in, own, sib_out, sib_in, far_out, far_in, att,
    kv_sem, xs, xr, ws, wr, zs, zr, os, orr, cs, cr, gs, gr, qsem, qr, ps_sem, pr_sem, ds, dr,
):
    n_hist = chips * CORES
    u = lax.axis_index("cand")
    h = lax.axis_index("hist")
    z = lax.div(h, CORES)
    c = lax.rem(h, CORES)
    sib = z * CORES + (1 - c)
    rows = inputs_hbm.shape[1]
    width = w_ref.shape[2]
    depth = w_ref.shape[1]
    features = inputs_hbm.shape[2]
    cands = rows * n_hist
    slots = order_ref.shape[1]
    tile = k_hbm.shape[1] // slots

    def chip_at(k):
        return lax.rem(z + k, chips)

    def same(k):
        return chip_at(k) * CORES + c

    def other(k):
        return chip_at(k) * CORES + (1 - c)

    def remote(src, dst, send, recv, hist_to, cand_to=None):
        return pltpu.make_async_remote_copy(
            src_ref=src, dst_ref=dst, send_sem=send, recv_sem=recv,
            device_id=(u if cand_to is None else cand_to, hist_to), device_id_type=MESH,
        )

    barrier = pltpu.get_barrier_semaphore()
    for i in range(1, n_hist):
        pl.semaphore_signal(
            barrier, inc=1, device_id=(u, lax.rem(h + i, n_hist)), device_id_type=MESH
        )
    for j in range(1, n_cand):
        pl.semaphore_signal(
            barrier, inc=1, device_id=(lax.rem(u + j, n_cand), h), device_id_type=MESH
        )
    stage_in = [
        pltpu.make_async_copy(src, dst, in_sem.at[i])
        for i, (src, dst) in enumerate(
            (
                (inputs_hbm, inputs_ref),
                (in_gain_hbm, in_gain_ref),
                (w_ref, wq.at[:, pl.ds(pl.multiple_of(u * depth, depth), depth)]),
                (wo_ref, wo.at[u, c, z]),
                (out_gain_hbm, out_gain_ref),
                (bias_hbm, bias_ref),
                (len_hbm, len_ref),
                (order_hbm, order_ref),
                (mask_hbm, mask_ref),
            )
        )
    ]
    for copy in stage_in:
        copy.start()
    key_copy = pltpu.make_async_copy(k_hbm.at[0], keys, kv_sem.at[0])
    value_copy = pltpu.make_async_copy(v_hbm.at[0], vals, kv_sem.at[1])
    key_copy.start()
    value_copy.start()

    stage_in[0].wait()
    stage_in[1].wait()
    normed = layer_norm(inputs_ref[0].astype(jnp.float32), in_gain_ref[...])

    def x_at(hh):
        return xn.at[pl.ds(pl.multiple_of(hh * rows, rows), rows)]

    x_at(h)[...] = normed.astype(jnp.bfloat16)

    def w_slot(i, uu):
        return wq.at[i, pl.ds(pl.multiple_of(uu * depth, depth), depth)]

    pl.semaphore_wait(barrier, n_hist - 1 + n_cand - 1)

    def w_copy(i, j):
        return remote(
            w_ref.at[i], w_slot(i, u), ws.at[i, j], wr.at[i, n_cand - j], h, lax.rem(u + j, n_cand)
        )

    def z_copy(k):
        return remote(wo_ref, wo.at[u, c, z], zs.at[k], zr.at[chips - k], same(k))

    def o_sib():
        return remote(wo.at[u, c], wo.at[u, c], os.at[0, 0], orr.at[0, 0], sib)

    def o_copy(j, k):
        slot = wo.at[u, c, chip_at(k)]
        return remote(
            wo_ref if k == 0 else slot, slot, os.at[j, k], orr.at[n_cand - j, k], h,
            lax.rem(u + j, n_cand),
        )

    def c_copy(j):
        uu = lax.rem(u + j, n_cand)
        return remote(wo.at[uu, c], wo.at[uu, c], cs.at[j], cr.at[j], sib)

    def direct(at, send, recv, k):
        if k == 0:
            return remote(at(h), at(h), send.at[0], recv.at[0], sib)
        return remote(at(h), at(h), send.at[k], recv.at[chips - k], same(k))

    def arrived(at, send, recv, hh, index):
        remote(at(hh), at(hh), send.at[index], recv.at[index], sib).wait_recv()

    def onward(at, send, recv, k):
        hh = same(k)
        return remote(at(hh), at(hh), send.at[chips + k], recv.at[chips + k], sib)

    for k in sorted(range(1, chips), key=lambda k: abs(2 * k - chips)):
        direct(x_at, xs, xr, k).start()
    direct(x_at, xs, xr, 0).start()
    for j in range(1, n_cand):
        w_copy(0, j).start()
    for j in range(1, n_cand):
        o_copy(j, 0).start()
    for k in range(1, chips):
        z_copy(k).start()
    for j in range(1, n_cand):
        w_copy(1, j).start()

    for k in range(1, chips):
        arrived(x_at, xs, xr, same(k), k)
        onward(x_at, xs, xr, k).start()
    for j in range(1, n_cand):
        w_copy(0, j).wait_recv()
    arrived(x_at, xs, xr, sib, 0)
    for k in range(1, chips):
        arrived(x_at, xs, xr, other(k), chips + k)

    stage_in[2].wait()
    half_query = 0.5 * jnp.dot(xn[...], wq[0], preferred_element_type=jnp.float32)
    score_scale = 0.5 / math.sqrt(features // bias_ref.shape[0])
    qs[h] = (silu_of_half(half_query) * score_scale).astype(jnp.bfloat16)

    def q_at(hh):
        return qs.at[hh]

    for k in sorted(range(1, chips), key=lambda k: abs(2 * k - chips)):
        direct(q_at, qsem, qr, k).start()
    direct(q_at, qsem, qr, 0).start()

    for k in range(1, chips):
        z_copy(chips - k).wait_recv()
        for j in range(1, n_cand):
            o_copy(j, k).start()
    stage_in[3].wait()
    o_sib().start()
    for j in range(1, n_cand):
        w_copy(1, j).wait_recv()
    gate_out[...] = (
        silu_of_half(0.5 * jnp.dot(xn[...], wq[1], preferred_element_type=jnp.float32))
        .astype(jnp.bfloat16)
        .reshape(n_hist, rows, width)
    )

    def g_copy(i):
        to = lax.rem(h + i, n_hist)
        return remote(gate_out.at[to], gate_in.at[h], gs.at[i], gr.at[n_hist - i], to)

    for i in range(1, n_hist):
        g_copy(i).start()
    gate_in[h] = gate_out[h]
    key_copy.wait()
    for copy in stage_in[4:]:
        copy.wait()
    value_copy.wait()
    for t in range(slots):
        limit = jnp.where(mask_ref[0, t] == 1, len_ref[0] - order_ref[0, t] * tile, 0)
        place = lax.broadcasted_iota(jnp.int32, (tile, width), 0)
        live = jnp.where(place < limit, 1.0, 0.0).astype(jnp.bfloat16)
        for n in range(features // width):
            part = (slice(t * tile, (t + 1) * tile), slice(n * width, (n + 1) * width))
            vals[part] = vals[part] * live

    heads_here = width * bias_ref.shape[0] // features
    head_dim = width // heads_here

    def block(p):
        columns = pl.ds(pl.multiple_of(p * width, width), width)
        query = qs[p]
        lane = lax.broadcasted_iota(jnp.int32, (cands, width), 1)
        result = None
        for j in range(heads_here):
            in_head = (lane >= j * head_dim) & (lane < (j + 1) * head_dim)
            head_mask = jnp.where(in_head, 1.0, 0.0).astype(jnp.bfloat16)
            query_head = query * head_mask
            total = jnp.zeros((cands, width), jnp.float32)
            for t in range(slots):
                events = slice(t * tile, (t + 1) * tile)
                half = lax.dot_general(
                    query_head, keys[events, columns], (((1,), (1,)), ((), ())),
                    preferred_element_type=jnp.float32,
                ) + 0.5 * bias_ref[p * heads_here + j, order_ref[0, t]]
                weights = silu_of_half(half).astype(jnp.bfloat16)
                total += jnp.dot(
                    weights, vals[events, columns], preferred_element_type=jnp.float32
                )
            result = total if result is None else jnp.where(in_head, total, result)
        return result

    def sib_copy(k):
        return remote(sib_out.at[k], sib_in.at[k], ps_sem.at[k], pr_sem.at[k], sib)

    def far_copy(k, i):
        return remote(
            far_out.at[k, :, chip_at(i)], far_in.at[chips - i, chip_at(k)],
            ds.at[k, i], dr.at[chips - i, chip_at(k)], same(i),
        )

    def keep(k, parity, p):
        result = block(p).reshape(chips, CORES, rows, width)
        for side in range(CORES):
            own[k, parity, :, side] = result[:, side]
        sib_out[k, parity] = own[k, parity, :, 1 - c].astype(jnp.bfloat16)

    def combine(k):
        sib_copy(k).wait_recv()
        both = own[k, :, :, c] + sib_in[k].astype(jnp.float32)
        own[k, :, :, c] = both
        far_out[k] = both.astype(jnp.bfloat16)
        for i in range(1, chips):
            far_copy(k, i).start()
        att[chip_at(k)] = own[k, :, z, c]

    def step(k, carry):
        keep(k, c, same(k))

        @pl.when(k < chips - 1)
        def _():
            arrived(q_at, qsem, qr, same(k + 1), k + 1)
            onward(q_at, qsem, qr, k + 1).start()

        @pl.when(k == 0)
        def _():
            arrived(q_at, qsem, qr, sib, 0)

        @pl.when(k > 0)
        def _():
            combine(k - 1)
            arrived(q_at, qsem, qr, other(k), chips + k)

        keep(k, 1 - c, other(k))
        sib_copy(k).start()
        return carry

    lax.fori_loop(0, chips, step, 0)
    combine(chips - 1)
    for j in range(1, n_cand):
        for k in range(chips):
            o_copy(n_cand - j, k).wait_recv()
        c_copy(j).start()

    for i in range(1, n_hist):
        g_copy(i).wait_recv()
    for i in range(1, chips):
        for k in range(chips):
            remote(
                far_out.at[0, :, 0], far_in.at[i, k], ds.at[0, i], dr.at[i, k], sib
            ).wait_recv()
    columns = []
    gate_columns = []
    for hh in range(n_hist):
        piece = att[hh // CORES, hh % CORES]
        for i in range(1, chips):
            piece = piece + far_in[i, hh // CORES, hh % CORES].astype(jnp.float32)
        columns.append(piece)
        gate_columns.append(gate_in[hh].astype(jnp.float32))
    attended = jnp.concatenate(columns, axis=1)
    gates = jnp.concatenate(gate_columns, axis=1)
    gated = (layer_norm(attended, out_gain_ref[...]) * gates).astype(jnp.bfloat16)
    sides = [
        jnp.concatenate(
            [
                gated[:, hh * width : (hh + 1) * width]
                for hh in range(side, n_hist, CORES)
            ],
            axis=1,
        )
        for side in range(CORES)
    ]
    wide = wo_ref.shape[1]
    o_sib().wait_recv()
    for j in range(1, n_cand):
        c_copy(j).wait_recv()
    for n in range(n_cand):
        part = slice(n * wide, (n + 1) * wide)
        total = inputs_ref[0, :, part].astype(jnp.float32)
        for side in range(CORES):
            total += jnp.dot(
                sides[side], wo[n, side].reshape(chips * width, wide),
                preferred_element_type=jnp.float32,
            )
        out_ref[0, :, part] = total.astype(jnp.bfloat16)

    for k in range(chips):
        direct(x_at, xs, xr, k).wait_send()
        direct(q_at, qsem, qr, k).wait_send()
        sib_copy(k).wait_send()
        if k > 0:
            onward(x_at, xs, xr, k).wait_send()
            onward(q_at, qsem, qr, k).wait_send()
            z_copy(k).wait_send()
            for q in range(chips):
                far_copy(q, k).wait_send()
    o_sib().wait_send()
    for j in range(1, n_cand):
        w_copy(0, j).wait_send()
        w_copy(1, j).wait_send()
        for k in range(chips):
            o_copy(j, k).wait_send()
        c_copy(j).wait_send()
    for i in range(1, n_hist):
        g_copy(i).wait_send()


def fused_shards(
    n_cand, n_hist, inputs, in_gain, w_qu, out_gain, w_out, hist_keys, hist_values, pos_bias,
    lengths, tile_order, tile_mask,
):
    chips = n_hist // CORES
    rows, features = inputs.shape[1:]
    depth, width = w_qu.shape[1:]
    cands = rows * n_hist
    events = hist_keys.shape[1]
    half, full = jnp.bfloat16, jnp.float32
    vmem = pl.BlockSpec(memory_space=pltpu.VMEM)
    hbm = pl.BlockSpec(memory_space=pltpu.HBM)
    dma = pltpu.SemaphoreType.DMA
    pieces = pltpu.VMEM((chips, CORES, chips, rows, width), half)
    return pl.pallas_call(
        functools.partial(fused, n_cand, chips),
        out_shape=pltpu.VMEM(inputs.shape, half),
        in_specs=[hbm] * 11,
        out_specs=vmem,
        scratch_shapes=[
            pltpu.VMEM(inputs.shape, half),
            pltpu.VMEM((1, features), full),
            pltpu.VMEM((1, features), full),
            pltpu.SMEM(pos_bias.shape, full),
            pltpu.SMEM(lengths.shape, jnp.int32),
            pltpu.SMEM(tile_order.shape, jnp.int32),
            pltpu.SMEM(tile_mask.shape, jnp.int32),
            dma((9,)),
            pltpu.VMEM((cands, features), half),
            pltpu.VMEM((2, depth * n_cand, width), half),
            pltpu.VMEM((n_cand, CORES, chips, width, w_out.shape[1]), half),
            pltpu.VMEM((events, features), half),
            pltpu.VMEM((events, features), half),
            pltpu.VMEM((n_hist, cands, width), half),
            pltpu.VMEM((n_hist, rows, width), half),
            pltpu.VMEM((n_hist, rows, width), half),
            pltpu.VMEM((chips, CORES, chips, CORES, rows, width), full),
            pieces, pieces, pieces,
            pltpu.VMEM((chips, chips, CORES, rows, width), half),
            pltpu.VMEM((chips, CORES, rows, width), full),
            dma((2,)),
            dma((2 * chips,)), dma((2 * chips,)),
            dma((2, n_cand)), dma((2, n_cand)),
            dma((chips,)), dma((chips,)),
            dma((n_cand, chips)), dma((n_cand, chips)),
            dma((n_cand,)), dma((n_cand,)),
            dma((n_hist,)), dma((n_hist,)),
            dma((2 * chips,)), dma((2 * chips,)),
            dma((chips,)), dma((chips,)),
            dma((chips, chips)), dma((chips, chips)),
        ],
        compiler_params=pltpu.CompilerParams(
            collective_id=0, has_side_effects=True, vmem_limit_bytes=60 * 1024 * 1024
        ),
    )(
        inputs, in_gain[None], w_qu, out_gain[None], w_out, hist_keys, hist_values, pos_bias,
        lengths, tile_order, tile_mask,
    )


def solution(mesh):
    n_cand, n_hist = mesh.shape["cand"], mesh.shape["hist"]

    def local(*arrays):
        depth, width = arrays[2].shape[1:]
        head_dim = arrays[0].shape[2] // arrays[7].shape[0]
        if n_hist % CORES == 0 and width % 128 == 0 and width % head_dim == 0 and depth % 16 == 0:
            return fused_shards(n_cand, n_hist, *arrays)
        return shards(*arrays)

    placed = (
        P("cand", "hist", None),
        P(),
        P(None, "cand", "hist"),
        P(),
        P("hist", "cand"),
        P("cand", "hist", None),
        P("cand", "hist", None),
        P(),
        P("cand"),
        P("cand", "hist"),
        P("cand", "hist"),
    )
    return jax.shard_map(
        local, mesh=mesh, in_specs=placed, out_specs=P("cand", "hist", None), check_vma=False
    )
```

```python
import functools
import math

import jax
import jax.numpy as jnp
from jax import lax
from jax.experimental import pallas as pl
from jax.experimental.pallas import tpu as pltpu
from jax.sharding import PartitionSpec as P

EPS = 1e-05


def layer_norm(values, gain_vector):
    row_mean = jnp.mean(values, axis=-1, keepdims=True)
    square = jnp.mean(values * values, axis=-1, keepdims=True)
    return (values - row_mean) * lax.rsqrt(square - row_mean * row_mean + EPS) * gain_vector


def attention(all_queries, hist_keys, hist_values, pos_bias, lengths, tile_order, tile_mask):
    cands = all_queries.shape[1]
    width = all_queries.shape[2]
    heads = pos_bias.shape[0]
    tiles_all = pos_bias.shape[1]
    slots = tile_order.shape[1]
    tile = hist_keys.shape[1] // slots
    head_dim = width // heads
    score_scale = 1.0 / math.sqrt(head_dim)
    tile_numbers = jnp.arange(tiles_all, dtype=jnp.int32)
    offsets = jnp.arange(tile, dtype=jnp.int32)

    def one_user(user_items):
        user_query, key_block, value_block, slot_order, slot_mask, length = user_items
        query_heads = user_query.reshape(cands, heads, head_dim)
        one_hot = (slot_order[:, None] == tile_numbers[None, :]).astype(jnp.float32)
        slot_bias = jnp.dot(one_hot, pos_bias.T, precision=lax.Precision.HIGHEST)
        summed = jnp.zeros((cands, heads, head_dim), jnp.float32)
        for slot_index in range(slots):
            key_tile = key_block[slot_index * tile : (slot_index + 1) * tile].reshape(
                tile, heads, head_dim
            )
            value_tile = value_block[slot_index * tile : (slot_index + 1) * tile].reshape(
                tile, heads, head_dim
            )
            positions = slot_order[slot_index] * tile + offsets
            is_live = ((slot_mask[slot_index] == 1) & (positions < length)).astype(jnp.float32)
            bias_row = slot_bias[slot_index]

            def compute(
                key_tile=key_tile, value_tile=value_tile, is_live=is_live, bias_row=bias_row
            ):
                scores = jnp.einsum(
                    "chd,ehd->che", query_heads, key_tile, preferred_element_type=jnp.float32
                )
                scores = scores * score_scale + bias_row[None, :, None]
                weights = (jax.nn.silu(scores) * is_live[None, None, :]).astype(jnp.bfloat16)
                return jnp.einsum(
                    "che,ehd->chd", weights, value_tile, preferred_element_type=jnp.float32
                )

            summed = summed + compute()
        return summed.reshape(cands, width)

    return lax.map(one_user, (all_queries, hist_keys, hist_values, tile_order, tile_mask, lengths))


def shards(
    inputs,
    in_gain,
    w_qu,
    out_gain,
    w_out,
    hist_keys,
    hist_values,
    pos_bias,
    lengths,
    tile_order,
    tile_mask,
):
    w_full, out_rows = (
        lax.all_gather(w_qu, "cand", axis=1, tiled=True),
        lax.all_gather(w_out, "cand", axis=1, tiled=True),
    )
    normed = layer_norm(inputs.astype(jnp.float32), in_gain).astype(jnp.bfloat16)
    projected = jnp.einsum(
        "ucd,jdk->ucjk",
        normed,
        lax.all_gather(w_full, "hist", axis=2, tiled=True),
        preferred_element_type=jnp.float32,
    )
    queries = jax.nn.silu(projected[:, :, 0]).astype(jnp.bfloat16)
    gates = jax.nn.silu(projected[:, :, 1])
    all_queries = lax.all_gather(queries, "hist", axis=1, tiled=True)
    attended = attention(
        all_queries, hist_keys, hist_values, pos_bias, lengths, tile_order, tile_mask
    )
    own_rows = lax.psum_scatter(
        attended.astype(jnp.bfloat16), "hist", scatter_dimension=1, tiled=True
    ).astype(jnp.float32)
    gated = (layer_norm(own_rows, out_gain) * gates).astype(jnp.bfloat16)
    projected_out = jnp.einsum(
        "uck,kd->ucd",
        gated,
        lax.all_gather(out_rows, "hist", axis=0, tiled=True),
        preferred_element_type=jnp.float32,
    )
    return (inputs.astype(jnp.float32) + projected_out).astype(jnp.bfloat16)


MESH = pl.DeviceIdType.MESH
CORES = 2


def silu_of_half(half):
    return half + half * jnp.tanh(half)


def fused(
    n_cand, chips, inputs_hbm, in_gain_hbm, w_ref, out_gain_hbm, wo_ref, k_hbm, v_hbm, bias_hbm,
    len_hbm, order_hbm, mask_hbm, out_ref,
    inputs_ref, in_gain_ref, out_gain_ref, bias_ref, len_ref, order_ref, mask_ref, in_sem, xn,
    wq, wo, keys, vals, vals_out, tab, tab_out, qs, gate_out, gate_in, part_out, part_in,
    k_own, v_own, v_other, ks, kr, vs, vr, ts, tr, xs, xr, fs, fr, ws, wr, zs, zr, os, orr, cs, cr,
    gs, gr, qsem, qr, ps, pr,
):
    n_hist = chips * CORES
    u = lax.axis_index("cand")
    h = lax.axis_index("hist")
    z = lax.div(h, CORES)
    c = lax.rem(h, CORES)
    sib = z * CORES + (1 - c)
    rows = inputs_hbm.shape[1]
    width = w_ref.shape[2]
    depth = w_ref.shape[1]
    features = inputs_hbm.shape[2]
    slots = order_ref.shape[1]
    events = k_hbm.shape[1]
    tile = events // slots
    pair = CORES * rows
    heads_here = width * bias_ref.shape[0] // features
    head_dim = width // heads_here

    inner = lax.rem(lax.div(z + 1, 2), 2)
    across = lax.rem(z + 2, chips)
    mirror = chips - 1 - z
    line = [
        z,
        z + 1 - 2 * lax.rem(z, 2),
        inner * mirror + (1 - inner) * across,
        inner * across + (1 - inner) * mirror,
    ]

    def line_at(k):
        place = line[chips - 1]
        for i in range(chips - 1):
            place = jnp.where(k == i, line[i], place)
        return place

    def chip_at(k):
        return lax.rem(z + k, chips)

    def remote(src, dst, send, recv, hist_to, cand_to=None):
        return pltpu.make_async_remote_copy(
            src_ref=src, dst_ref=dst, send_sem=send, recv_sem=recv,
            device_id=(u if cand_to is None else cand_to, hist_to), device_id_type=MESH,
        )

    stage_in = [
        pltpu.make_async_copy(src, dst, in_sem.at[i])
        for i, (src, dst) in enumerate(
            (
                (inputs_hbm, inputs_ref),
                (in_gain_hbm, in_gain_ref),
                (w_ref, wq.at[:, pl.ds(pl.multiple_of(u * depth, depth), depth)]),
                (wo_ref, wo.at[u, c, z]),
                (out_gain_hbm, out_gain_ref),
                (bias_hbm, bias_ref),
                (len_hbm, len_ref),
                (order_hbm, order_ref),
                (mask_hbm, mask_ref),
            )
        )
    ]
    stage_in[0].start()
    stage_in[1].start()
    barrier = pltpu.get_barrier_semaphore()
    for i in range(1, n_hist):
        pl.semaphore_signal(
            barrier, inc=1, device_id=(u, lax.rem(h + i, n_hist)), device_id_type=MESH
        )
    for j in range(1, n_cand):
        pl.semaphore_signal(
            barrier, inc=1, device_id=(lax.rem(u + j, n_cand), h), device_id_type=MESH
        )
    for copy in stage_in[2:]:
        copy.start()

    def columns_of(ref, b, core):
        return ref.at[0, :, pl.ds(pl.multiple_of((b * CORES + core) * width, width), width)]

    def own_keys(b):
        return pltpu.make_async_copy(columns_of(k_hbm, b, c), keys.at[b, c], k_own.at[b])

    def own_values(b):
        return pltpu.make_async_copy(columns_of(v_hbm, b, c), vals.at[b, c], v_own.at[b])

    def other_values(b):
        return pltpu.make_async_copy(columns_of(v_hbm, b, 1 - c), vals_out.at[b], v_other.at[b])

    for b in range(chips):
        other_values(b).start()
    for b in range(chips):
        own_values(b).start()
        own_keys(b).start()

    stage_in[0].wait()
    stage_in[1].wait()
    normed = layer_norm(inputs_ref[0].astype(jnp.float32), in_gain_ref[...])

    def x_at(hh):
        return xn.at[pl.ds(pl.multiple_of(hh * rows, rows), rows)]

    x_at(h)[...] = normed.astype(jnp.bfloat16)
    pl.semaphore_wait(barrier, n_hist - 1 + n_cand - 1)

    def w_slot(i, uu):
        return wq.at[i, pl.ds(pl.multiple_of(uu * depth, depth), depth)]

    def w_copy(i, j):
        return remote(
            w_ref.at[i], w_slot(i, u), ws.at[i, j], wr.at[i, n_cand - j], h, lax.rem(u + j, n_cand)
        )

    def z_copy(k):
        return remote(wo_ref, wo.at[u, c, z], zs.at[k], zr.at[z], line[k] * CORES + c)

    def z_from(k):
        slot = wo.at[u, c, line[k]]
        return remote(slot, slot, zs.at[k], zr.at[line[k]], sib)

    def z_onward(k):
        slot = wo.at[u, c, line[k]]
        return remote(slot, slot, zs.at[3 * (k - 2)], zr.at[line[k]], line[1] * CORES + c)

    def o_sib():
        return remote(wo.at[u, c], wo.at[u, c], os.at[0, 0], orr.at[0, 0], sib)

    def o_copy(j, k):
        slot = wo.at[u, c, line[k]]
        return remote(
            wo_ref if k == 0 else slot, slot, os.at[j, k], orr.at[n_cand - j, k], h,
            lax.rem(u + j, n_cand),
        )

    def c_copy(j):
        uu = lax.rem(u + j, n_cand)
        return remote(wo.at[uu, c], wo.at[uu, c], cs.at[j], cr.at[j], sib)

    def x_copy(zz):
        return remote(x_at(h), x_at(h), xs.at[zz], xr.at[z], zz * CORES + c)

    def x_from(zz):
        hh = zz * CORES + c
        return remote(x_at(hh), x_at(hh), xs.at[zz], xr.at[zz], sib)

    def x_onward(zz):
        hh = zz * CORES + c
        return remote(x_at(hh), x_at(hh), fs.at[zz], fr.at[zz], sib)

    def x_across(zz):
        hh = zz * CORES + (1 - c)
        return remote(x_at(hh), x_at(hh), fs.at[zz], fr.at[zz], sib)

    def key_copy(b):
        return remote(columns_of(k_hbm, b, 1 - c), keys.at[b, c], ks.at[b], kr.at[b], sib)

    def value_copy(b):
        return remote(vals_out.at[b], vals.at[b, c], vs.at[b], vr.at[b], sib)

    def key_from(b):
        return remote(keys.at[b, 1 - c], keys.at[b, 1 - c], ks.at[b], kr.at[b], sib)

    def value_from(b):
        return remote(vals.at[b, 1 - c], vals.at[b, 1 - c], vs.at[b], vr.at[b], sib)

    def tab_copy():
        return remote(tab_out, tab.at[c], ts.at[0], tr.at[0], sib)

    def tab_from():
        return remote(tab_out, tab.at[1 - c], ts.at[0], tr.at[0], sib)

    for k in reversed(range(1, chips)):
        x_copy(line[k]).start()
    x_onward(z).start()
    for j in range(1, n_cand):
        w_copy(0, j).start()
    z_copy(1).start()
    z_copy(2).start()
    for j in range(1, n_cand):
        o_copy(j, 0).start()
    for j in range(1, n_cand):
        w_copy(1, j).start()
    for b in range(chips):
        key_copy(b).start()

    for copy in stage_in[4:]:
        copy.wait()
    for t in range(slots):
        for b in range(chips):
            for j in range(heads_here):
                for core in range(CORES):
                    head = (b * CORES + core) * heads_here + j
                    row = jnp.full((1, width), 0.5 * bias_ref[head, order_ref[0, t]], jnp.float32)
                    is_own = c == core

                    @pl.when(is_own)
                    def _(t=t, b=b, j=j, row=row):
                        tab[c, t, b, j : j + 1] = row

                    @pl.when(jnp.logical_not(is_own))
                    def _(t=t, b=b, j=j, row=row):
                        tab_out[t, b, j : j + 1] = row
    tab_copy().start()
    live = []
    for t in range(slots):
        limit = jnp.where(mask_ref[0, t] == 1, len_ref[0] - order_ref[0, t] * tile, 0)
        place = lax.broadcasted_iota(jnp.int32, (tile, width), 0)
        live.append(jnp.where(place < limit, 1.0, 0.0).astype(jnp.bfloat16))
    for b in range(chips):
        other_values(b).wait()
        for t in range(slots):
            part = slice(t * tile, (t + 1) * tile)
            vals_out[b, part] = vals_out[b, part] * live[t]
        value_copy(b).start()
    for b in range(chips):
        own_values(b).wait()
        for t in range(slots):
            part = slice(t * tile, (t + 1) * tile)
            vals[b, c, part] = vals[b, c, part] * live[t]

    for k in range(1, chips):
        x_from(line[k]).wait_recv()
        x_onward(line[k]).start()
    for j in range(1, n_cand):
        w_copy(0, j).wait_recv()
    stage_in[2].wait()
    score_scale = 0.5 / math.sqrt(head_dim)

    def piece_at(b, zz):
        return qs.at[b, pl.ds(pl.multiple_of(zz * pair, pair), pair)]

    def q_copy(zz, k):
        piece = piece_at(z, zz)
        return remote(piece, piece, qsem.at[zz, line[k]], qr.at[z, zz], line[k] * CORES + c)

    for k in range(chips):
        zz = line[k]
        x_across(zz).wait_recv()
        x_piece = xn[pl.ds(pl.multiple_of(zz * pair, pair), pair)]
        half_query = 0.5 * jnp.dot(x_piece, wq[0], preferred_element_type=jnp.float32)
        piece_at(z, zz)[...] = (silu_of_half(half_query) * score_scale).astype(jnp.bfloat16)
        for i in reversed(range(1, chips)):
            q_copy(zz, i).start()

    def g_copy(i):
        to = lax.rem(h + i, n_hist)
        return remote(gate_out.at[to], gate_in.at[h], gs.at[i], gr.at[n_hist - i], to)

    tab_from().wait_recv()
    for b in range(chips):
        own_keys(b).wait()
        key_from(b).wait_recv()
        value_from(b).wait_recv()

    def attend(b, places):
        query = jnp.concatenate([piece_at(b, zz)[...] for zz in places], axis=0)
        count = query.shape[0]
        lane = lax.broadcasted_iota(jnp.int32, (count, width), 1)
        in_head = [(lane >= j * head_dim) & (lane < (j + 1) * head_dim) for j in range(heads_here)]
        stack = jnp.concatenate(
            [query * jnp.where(at, 1.0, 0.0).astype(jnp.bfloat16) for at in in_head], axis=0
        )
        total = None
        for core in range(CORES):
            for t in range(slots):
                part = slice(t * tile, (t + 1) * tile)
                scores = lax.dot_general(
                    stack, keys[b, core, part], (((1,), (1,)), ((), ())),
                    preferred_element_type=jnp.float32,
                )
                bias = jnp.concatenate([tab[core, t, b]] * (tile // width), axis=1)
                half = jnp.concatenate(
                    [
                        scores[j * count : (j + 1) * count] + bias[j : j + 1]
                        for j in range(heads_here)
                    ],
                    axis=0,
                )
                weights = silu_of_half(half).astype(jnp.bfloat16)
                here = jnp.dot(weights, vals[b, core, part], preferred_element_type=jnp.float32)
                total = here if total is None else total + here
        result = total[:count]
        for j in range(1, heads_here):
            result = jnp.where(in_head[j], total[j * count : (j + 1) * count], result)
        return result.reshape(len(places), CORES, rows, width).astype(jnp.bfloat16)

    def p_copy(b, to):
        return remote(part_out.at[b, to], part_in.at[h, b], ps.at[b, to], pr.at[h, b], to)

    def step(k, carry):
        b = line_at(k)

        @pl.when(k > 0)
        def _():
            for zz in range(chips):
                remote(
                    piece_at(b, zz), piece_at(b, zz), qsem.at[zz, 0], qr.at[b, zz], sib
                ).wait_recv()

        for group in ((3, 2), (1, 0)):
            result = attend(b, [line[i] for i in group])
            for n, i in enumerate(group):
                part_out[b, pl.ds(line[i] * CORES, CORES)] = result[n]
                if i > 0:
                    for core in range(CORES):
                        p_copy(b, line[i] * CORES + core).start()
                else:
                    p_copy(b, sib).start()
                    part_in[h, b] = part_out[b, h]

        @pl.when(k == 0)
        def _():
            for j in range(1, n_cand):
                w_copy(1, j).wait_recv()
            gate_out[...] = (
                silu_of_half(0.5 * jnp.dot(xn[...], wq[1], preferred_element_type=jnp.float32))
                .astype(jnp.bfloat16)
                .reshape(n_hist, rows, width)
            )
            for i in range(1, n_hist):
                g_copy(i).start()
            gate_in[h] = gate_out[h]

        @pl.when((k == 1) & (inner == 0))
        def _():
            for i in (2, 3):
                z_from(i).wait_recv()
                for j in range(1, n_cand):
                    o_copy(j, i).start()

        return carry

    z_from(1).wait_recv()
    for j in range(1, n_cand):
        o_copy(j, 1).start()

    @pl.when(inner == 1)
    def _():
        for k in (2, 3):
            z_from(k).wait_recv()
            z_onward(k).start()
            for j in range(1, n_cand):
                o_copy(j, k).start()

    lax.fori_loop(0, chips, step, 0)
    stage_in[3].wait()
    o_sib().start()
    for j in range(1, n_cand):
        for k in range(chips):
            o_copy(n_cand - j, k).wait_recv()
        c_copy(j).start()

    for i in range(1, n_hist):
        g_copy(i).wait_recv()
    for i in range(1, n_hist):
        hh = lax.rem(h + i, n_hist)
        for b in range(chips):
            remote(part_out.at[b, 0], part_in.at[hh, b], ps.at[b, 0], pr.at[hh, b], sib).wait_recv()
    columns = []
    gate_columns = []
    for hh in range(n_hist):
        b, core = hh // CORES, hh % CORES
        piece = part_in[core, b].astype(jnp.float32)
        for i in range(1, chips):
            piece = piece + part_in[i * CORES + core, b].astype(jnp.float32)
        columns.append(piece)
        gate_columns.append(gate_in[hh].astype(jnp.float32))
    attended = jnp.concatenate(columns, axis=1)
    gates = jnp.concatenate(gate_columns, axis=1)
    gated = (layer_norm(attended, out_gain_ref[...]) * gates).astype(jnp.bfloat16)
    sides = [
        jnp.concatenate(
            [gated[:, hh * width : (hh + 1) * width] for hh in range(side, n_hist, CORES)], axis=1
        )
        for side in range(CORES)
    ]
    wide = wo_ref.shape[1]
    o_sib().wait_recv()
    for j in range(1, n_cand):
        c_copy(j).wait_recv()
    for n in range(n_cand):
        part = slice(n * wide, (n + 1) * wide)
        total = inputs_ref[0, :, part].astype(jnp.float32)
        for side in range(CORES):
            total += jnp.dot(
                sides[side], wo[n, side].reshape(chips * width, wide),
                preferred_element_type=jnp.float32,
            )
        out_ref[0, :, part] = total.astype(jnp.bfloat16)

    tab_copy().wait_send()
    for k in range(chips):
        x_onward(line[k]).wait_send()
        key_copy(k).wait_send()
        value_copy(k).wait_send()
        p_copy(k, sib).wait_send()
        if k > 0:
            x_copy(line[k]).wait_send()
            for b in range(chips):
                q_copy(b, k).wait_send()
                for core in range(CORES):
                    p_copy(b, line[k] * CORES + core).wait_send()
    o_sib().wait_send()
    z_copy(1).wait_send()
    z_copy(2).wait_send()

    @pl.when(inner == 1)
    def _():
        for k in (2, 3):
            z_onward(k).wait_send()

    for j in range(1, n_cand):
        w_copy(0, j).wait_send()
        w_copy(1, j).wait_send()
        for k in range(chips):
            o_copy(j, k).wait_send()
        c_copy(j).wait_send()
    for i in range(1, n_hist):
        g_copy(i).wait_send()


def fused_shards(
    n_cand, n_hist, inputs, in_gain, w_qu, out_gain, w_out, hist_keys, hist_values, pos_bias,
    lengths, tile_order, tile_mask,
):
    chips = n_hist // CORES
    rows, features = inputs.shape[1:]
    depth, width = w_qu.shape[1:]
    cands = rows * n_hist
    events = hist_keys.shape[1]
    slots = tile_order.shape[1]
    heads_here = width * pos_bias.shape[0] // features
    half, full = jnp.bfloat16, jnp.float32
    vmem = pl.BlockSpec(memory_space=pltpu.VMEM)
    hbm = pl.BlockSpec(memory_space=pltpu.HBM)
    dma = pltpu.SemaphoreType.DMA
    return pl.pallas_call(
        functools.partial(fused, n_cand, chips),
        out_shape=pltpu.VMEM(inputs.shape, half),
        in_specs=[hbm] * 11,
        out_specs=vmem,
        scratch_shapes=[
            pltpu.VMEM(inputs.shape, half),
            pltpu.VMEM((1, features), full),
            pltpu.VMEM((1, features), full),
            pltpu.SMEM(pos_bias.shape, full),
            pltpu.SMEM(lengths.shape, jnp.int32),
            pltpu.SMEM(tile_order.shape, jnp.int32),
            pltpu.SMEM(tile_mask.shape, jnp.int32),
            dma((9,)),
            pltpu.VMEM((cands, features), half),
            pltpu.VMEM((2, depth * n_cand, width), half),
            pltpu.VMEM((n_cand, CORES, chips, width, w_out.shape[1]), half),
            pltpu.VMEM((chips, CORES, events, width), half),
            pltpu.VMEM((chips, CORES, events, width), half),
            pltpu.VMEM((chips, events, width), half),
            pltpu.VMEM((CORES, slots, chips, heads_here, width), full),
            pltpu.VMEM((slots, chips, heads_here, width), full),
            pltpu.VMEM((chips, cands, width), half),
            pltpu.VMEM((n_hist, rows, width), half),
            pltpu.VMEM((n_hist, rows, width), half),
            pltpu.VMEM((chips, n_hist, rows, width), half),
            pltpu.VMEM((n_hist, chips, rows, width), half),
            dma((chips,)), dma((chips,)), dma((chips,)),
            dma((chips,)), dma((chips,)),
            dma((chips,)), dma((chips,)),
            dma((1,)), dma((1,)),
            dma((chips,)), dma((chips,)),
            dma((chips,)), dma((chips,)),
            dma((2, n_cand)), dma((2, n_cand)),
            dma((chips,)), dma((chips,)),
            dma((n_cand, chips)), dma((n_cand, chips)),
            dma((n_cand,)), dma((n_cand,)),
            dma((n_hist,)), dma((n_hist,)),
            dma((chips, chips)), dma((chips, chips)),
            dma((chips, n_hist)), dma((n_hist, chips)),
        ],
        compiler_params=pltpu.CompilerParams(
            collective_id=0, has_side_effects=True, vmem_limit_bytes=60 * 1024 * 1024
        ),
    )(
        inputs, in_gain[None], w_qu, out_gain[None], w_out, hist_keys, hist_values, pos_bias,
        lengths, tile_order, tile_mask,
    )


def solution(mesh):
    n_cand, n_hist = mesh.shape["cand"], mesh.shape["hist"]

    def local(*arrays):
        depth, width = arrays[2].shape[1:]
        head_dim = arrays[0].shape[2] // arrays[7].shape[0]
        fits = n_hist == 4 * CORES and width % 128 == 0 and width % head_dim == 0
        if fits and depth % 16 == 0 and arrays[0].shape[2] == width * n_hist:
            return fused_shards(n_cand, n_hist, *arrays)
        return shards(*arrays)

    placed = (
        P("cand", "hist", None),
        P(),
        P(None, "cand", "hist"),
        P(),
        P("hist", "cand"),
        P("cand", "hist", None),
        P("cand", "hist", None),
        P(),
        P("cand"),
        P("cand", "hist"),
        P("cand", "hist"),
    )
    return jax.shard_map(
        local, mesh=mesh, in_specs=placed, out_specs=P("cand", "hist", None), check_vma=False
    )
```

```python
import functools
import math

import jax
import jax.numpy as jnp
from jax import lax
from jax.experimental import pallas as pl
from jax.experimental.pallas import tpu as pltpu
from jax.sharding import PartitionSpec as P

EPS = 1e-05


def layer_norm(values, gain_vector):
    row_mean = jnp.mean(values, axis=-1, keepdims=True)
    square = jnp.mean(values * values, axis=-1, keepdims=True)
    return (values - row_mean) * lax.rsqrt(square - row_mean * row_mean + EPS) * gain_vector


def attention(all_queries, hist_keys, hist_values, pos_bias, lengths, tile_order, tile_mask):
    cands = all_queries.shape[1]
    width = all_queries.shape[2]
    heads = pos_bias.shape[0]
    tiles_all = pos_bias.shape[1]
    slots = tile_order.shape[1]
    tile = hist_keys.shape[1] // slots
    head_dim = width // heads
    score_scale = 1.0 / math.sqrt(head_dim)
    tile_numbers = jnp.arange(tiles_all, dtype=jnp.int32)
    offsets = jnp.arange(tile, dtype=jnp.int32)

    def one_user(user_items):
        user_query, key_block, value_block, slot_order, slot_mask, length = user_items
        query_heads = user_query.reshape(cands, heads, head_dim)
        one_hot = (slot_order[:, None] == tile_numbers[None, :]).astype(jnp.float32)
        slot_bias = jnp.dot(one_hot, pos_bias.T, precision=lax.Precision.HIGHEST)
        summed = jnp.zeros((cands, heads, head_dim), jnp.float32)
        for slot_index in range(slots):
            key_tile = key_block[slot_index * tile : (slot_index + 1) * tile].reshape(
                tile, heads, head_dim
            )
            value_tile = value_block[slot_index * tile : (slot_index + 1) * tile].reshape(
                tile, heads, head_dim
            )
            positions = slot_order[slot_index] * tile + offsets
            is_live = ((slot_mask[slot_index] == 1) & (positions < length)).astype(jnp.float32)
            bias_row = slot_bias[slot_index]

            def compute(
                key_tile=key_tile, value_tile=value_tile, is_live=is_live, bias_row=bias_row
            ):
                scores = jnp.einsum(
                    "chd,ehd->che", query_heads, key_tile, preferred_element_type=jnp.float32
                )
                scores = scores * score_scale + bias_row[None, :, None]
                weights = (jax.nn.silu(scores) * is_live[None, None, :]).astype(jnp.bfloat16)
                return jnp.einsum(
                    "che,ehd->chd", weights, value_tile, preferred_element_type=jnp.float32
                )

            summed = summed + compute()
        return summed.reshape(cands, width)

    return lax.map(one_user, (all_queries, hist_keys, hist_values, tile_order, tile_mask, lengths))


def shards(
    inputs,
    in_gain,
    w_qu,
    out_gain,
    w_out,
    hist_keys,
    hist_values,
    pos_bias,
    lengths,
    tile_order,
    tile_mask,
):
    w_full, out_rows = (
        lax.all_gather(w_qu, "cand", axis=1, tiled=True),
        lax.all_gather(w_out, "cand", axis=1, tiled=True),
    )
    normed = layer_norm(inputs.astype(jnp.float32), in_gain).astype(jnp.bfloat16)
    projected = jnp.einsum(
        "ucd,jdk->ucjk",
        normed,
        lax.all_gather(w_full, "hist", axis=2, tiled=True),
        preferred_element_type=jnp.float32,
    )
    queries = jax.nn.silu(projected[:, :, 0]).astype(jnp.bfloat16)
    gates = jax.nn.silu(projected[:, :, 1])
    all_queries = lax.all_gather(queries, "hist", axis=1, tiled=True)
    attended = attention(
        all_queries, hist_keys, hist_values, pos_bias, lengths, tile_order, tile_mask
    )
    own_rows = lax.psum_scatter(
        attended.astype(jnp.bfloat16), "hist", scatter_dimension=1, tiled=True
    ).astype(jnp.float32)
    gated = (layer_norm(own_rows, out_gain) * gates).astype(jnp.bfloat16)
    projected_out = jnp.einsum(
        "uck,kd->ucd",
        gated,
        lax.all_gather(out_rows, "hist", axis=0, tiled=True),
        preferred_element_type=jnp.float32,
    )
    return (inputs.astype(jnp.float32) + projected_out).astype(jnp.bfloat16)


MESH = pl.DeviceIdType.MESH
CORES = 2


def silu_of_half(half):
    return half + half * jnp.tanh(half)


def fused(
    n_cand, chips, inputs_hbm, in_gain_hbm, w_ref, out_gain_hbm, wo_ref, k_hbm, v_hbm, bias_hbm,
    len_hbm, order_hbm, mask_hbm, out_ref,
    inputs_ref, in_gain_ref, out_gain_ref, bias_ref, len_ref, order_ref, mask_ref, in_sem, xn,
    wq, wo, keys, vals, vals_out, tab, tab_out, qs, q_out, gate_out, gate_in, part_out, part_in,
    k_own, v_own, v_other, ks, kr, vs, vr, ts, tr, xs, xr, fs, fr, ws, wr, zs, zr, os, orr, cs, cr,
    gs, gr, qsem, qr, ps, pr, xf, qf,
):
    n_hist = chips * CORES
    u = lax.axis_index("cand")
    h = lax.axis_index("hist")
    z = lax.div(h, CORES)
    c = lax.rem(h, CORES)
    sib = z * CORES + (1 - c)
    rows = inputs_hbm.shape[1]
    width = w_ref.shape[2]
    depth = w_ref.shape[1]
    features = inputs_hbm.shape[2]
    slots = order_ref.shape[1]
    events = k_hbm.shape[1]
    tile = events // slots
    pair = CORES * rows
    heads_here = width * bias_ref.shape[0] // features
    head_dim = width // heads_here

    inner = lax.rem(lax.div(z + 1, 2), 2)
    across = lax.rem(z + 2, chips)
    mirror = chips - 1 - z
    line = [
        z,
        z + 1 - 2 * lax.rem(z, 2),
        inner * mirror + (1 - inner) * across,
        inner * across + (1 - inner) * mirror,
    ]

    def line_at(k):
        place = line[chips - 1]
        for i in range(chips - 1):
            place = jnp.where(k == i, line[i], place)
        return place

    def chip_at(k):
        return lax.rem(z + k, chips)

    def remote(src, dst, send, recv, hist_to, cand_to=None):
        return pltpu.make_async_remote_copy(
            src_ref=src, dst_ref=dst, send_sem=send, recv_sem=recv,
            device_id=(u if cand_to is None else cand_to, hist_to), device_id_type=MESH,
        )

    mine = pl.ds(pl.multiple_of(c * width, width), width)
    theirs = pl.ds(pl.multiple_of((1 - c) * width, width), width)
    stage_in = [
        pltpu.make_async_copy(src, dst, in_sem.at[i])
        for i, (src, dst) in enumerate(
            (
                (inputs_hbm, inputs_ref),
                (in_gain_hbm, in_gain_ref),
                (w_ref, wq.at[:, pl.ds(pl.multiple_of(u * depth, depth), depth), mine]),
                (wo_ref, wo.at[u, c, z]),
                (out_gain_hbm, out_gain_ref),
                (bias_hbm, bias_ref),
                (len_hbm, len_ref),
                (order_hbm, order_ref),
                (mask_hbm, mask_ref),
            )
        )
    ]
    stage_in[0].start()
    stage_in[1].start()
    barrier = pltpu.get_barrier_semaphore()
    for i in range(1, n_hist):
        pl.semaphore_signal(
            barrier, inc=1, device_id=(u, lax.rem(h + i, n_hist)), device_id_type=MESH
        )
    for j in range(1, n_cand):
        pl.semaphore_signal(
            barrier, inc=1, device_id=(lax.rem(u + j, n_cand), h), device_id_type=MESH
        )
    for copy in stage_in[2:]:
        copy.start()

    def columns_of(ref, b, core):
        return ref.at[0, :, pl.ds(pl.multiple_of((b * CORES + core) * width, width), width)]

    def own_keys(b):
        return pltpu.make_async_copy(columns_of(k_hbm, b, c), keys.at[b, c], k_own.at[b])

    def own_values(b):
        return pltpu.make_async_copy(columns_of(v_hbm, b, c), vals.at[b, c], v_own.at[b])

    def other_values(b):
        return pltpu.make_async_copy(columns_of(v_hbm, b, 1 - c), vals_out.at[b], v_other.at[b])

    for b in range(chips):
        other_values(b).start()
    for b in range(chips):
        own_values(b).start()
        own_keys(b).start()

    stage_in[0].wait()
    stage_in[1].wait()
    normed = layer_norm(inputs_ref[0].astype(jnp.float32), in_gain_ref[...])

    def x_at(zz):
        return xn.at[pl.ds(pl.multiple_of(zz * rows, rows), rows)]

    x_at(z)[...] = normed.astype(jnp.bfloat16)
    pl.semaphore_wait(barrier, n_hist - 1 + n_cand - 1)

    def w_slot(i, uu):
        return wq.at[i, pl.ds(pl.multiple_of(uu * depth, depth), depth), mine]

    def w_copy(i, j):
        return remote(
            w_ref.at[i], w_slot(i, u), ws.at[i, j], wr.at[i, n_cand - j], h, lax.rem(u + j, n_cand)
        )

    def w_onward(i, j):
        slot = w_slot(i, lax.rem(u + j, n_cand))
        return remote(slot, slot, fs.at[i, j], fr.at[i, j], sib)

    def w_across(i, j):
        uu = lax.rem(u + j, n_cand)
        slot = wq.at[i, pl.ds(pl.multiple_of(uu * depth, depth), depth), theirs]
        return remote(slot, slot, fs.at[i, j], fr.at[i, j], sib)

    def w_gather(i):
        for j in range(1, n_cand):
            w_copy(i, n_cand - j).wait_recv()
            w_onward(i, j).start()

    def z_copy(k):
        return remote(wo_ref, wo.at[u, c, z], zs.at[k], zr.at[z], line[k] * CORES + c)

    def z_from(k):
        slot = wo.at[u, c, line[k]]
        return remote(slot, slot, zs.at[k], zr.at[line[k]], sib)

    def z_onward(k):
        slot = wo.at[u, c, line[k]]
        return remote(slot, slot, zs.at[3 * (k - 2)], zr.at[line[k]], line[1] * CORES + c)

    def o_sib():
        return remote(wo.at[u, c], wo.at[u, c], os.at[0, 0], orr.at[0, 0], sib)

    def o_copy(j, k):
        slot = wo.at[u, c, line[k]]
        return remote(
            wo_ref if k == 0 else slot, slot, os.at[j, k], orr.at[n_cand - j, k], h,
            lax.rem(u + j, n_cand),
        )

    def c_copy(j):
        uu = lax.rem(u + j, n_cand)
        return remote(wo.at[uu, c], wo.at[uu, c], cs.at[j], cr.at[j], sib)

    def x_copy(zz):
        return remote(x_at(z), x_at(z), xs.at[zz], xr.at[z], zz * CORES + c)

    def x_from(zz):
        return remote(x_at(zz), x_at(zz), xs.at[zz], xr.at[zz], sib)

    def x_forward(k):
        return remote(
            x_at(line[k]), x_at(line[k]), xf.at[k], xr.at[line[k]], line[1] * CORES + c
        )

    def key_copy(b):
        return remote(columns_of(k_hbm, b, 1 - c), keys.at[b, c], ks.at[b], kr.at[b], sib)

    def value_copy(b):
        return remote(vals_out.at[b], vals.at[b, c], vs.at[b], vr.at[b], sib)

    def key_from(b):
        return remote(keys.at[b, 1 - c], keys.at[b, 1 - c], ks.at[b], kr.at[b], sib)

    def value_from(b):
        return remote(vals.at[b, 1 - c], vals.at[b, 1 - c], vs.at[b], vr.at[b], sib)

    def tab_copy():
        return remote(tab_out, tab.at[c], ts.at[0], tr.at[0], sib)

    def tab_from():
        return remote(tab_out, tab.at[1 - c], ts.at[0], tr.at[0], sib)

    for j in range(1, n_cand):
        w_copy(0, j).start()
    for k in (2, 1):
        x_copy(line[k]).start()
    z_copy(1).start()
    z_copy(2).start()
    for j in range(1, n_cand):
        o_copy(j, 0).start()
    for j in range(1, n_cand):
        w_copy(1, j).start()
    stage_in[2].wait()
    w_onward(0, 0).start()
    w_onward(1, 0).start()
    for b in range(chips):
        key_copy(b).start()

    for copy in stage_in[4:]:
        copy.wait()
    for t in range(slots):
        for b in range(chips):
            for j in range(heads_here):
                for core in range(CORES):
                    head = (b * CORES + core) * heads_here + j
                    row = jnp.full((1, width), 0.5 * bias_ref[head, order_ref[0, t]], jnp.float32)
                    is_own = c == core

                    @pl.when(is_own)
                    def _(t=t, b=b, j=j, row=row):
                        tab[c, t, b, j : j + 1] = row

                    @pl.when(jnp.logical_not(is_own))
                    def _(t=t, b=b, j=j, row=row):
                        tab_out[t, b, j : j + 1] = row
    tab_copy().start()
    live = []
    for t in range(slots):
        limit = jnp.where(mask_ref[0, t] == 1, len_ref[0] - order_ref[0, t] * tile, 0)
        place = lax.broadcasted_iota(jnp.int32, (tile, width), 0)
        live.append(jnp.where(place < limit, 1.0, 0.0).astype(jnp.bfloat16))
    for b in range(chips):
        other_values(b).wait()
        for t in range(slots):
            part = slice(t * tile, (t + 1) * tile)
            vals_out[b, part] = vals_out[b, part] * live[t]
        value_copy(b).start()
    for b in range(chips):
        own_values(b).wait()
        for t in range(slots):
            part = slice(t * tile, (t + 1) * tile)
            vals[b, c, part] = vals[b, c, part] * live[t]

    @pl.when(inner == 1)
    def _():
        for k in (2, 3):
            x_from(line[k]).wait_recv()
            x_forward(k).start()

    w_gather(0)
    score_scale = 0.5 / math.sqrt(head_dim)
    near = lax.div(z, 2)

    def half_at(b, core, side):
        return qs.at[b, core, pl.ds(side * 2, 2)]

    def q_out_at(side):
        return q_out.at[pl.ds(side * 2, 2)]

    def q_copy(side, k):
        piece = half_at(z, c, side)
        return remote(piece, piece, qsem.at[k], qr.at[z], line[k] * CORES + c)

    def q_cross(side, k):
        return remote(
            q_out_at(side), half_at(z, c, side), qf.at[k], qr.at[z], line[k] * CORES + (1 - c)
        )

    def query(side):
        block = xn[pl.ds(pl.multiple_of(side * pair, pair), pair)]
        half_query = 0.5 * jnp.dot(block, wq[0], preferred_element_type=jnp.float32)
        made = (silu_of_half(half_query) * score_scale).astype(jnp.bfloat16)
        parts = [
            made[:, core * width : (core + 1) * width].reshape(2, rows, width)
            for core in range(CORES)
        ]
        half_at(z, c, side)[...] = jnp.where(c == 0, parts[0], parts[1])
        q_out_at(side)[...] = jnp.where(c == 0, parts[1], parts[0])
        for k in reversed(range(1, chips)):
            q_copy(side, k).start()
            q_cross(side, k).start()
        q_cross(side, 0).start()

    for j in range(n_cand):
        w_across(0, j).wait_recv()
    x_from(line[1]).wait_recv()
    query(near)

    @pl.when(inner == 0)
    def _():
        for k in (2, 3):
            x_from(line[k]).wait_recv()

    query(1 - near)

    def g_copy(k):
        return remote(gate_out.at[line[k]], gate_in.at[z], gs.at[k], gr.at[z], line[k] * CORES + c)

    def g_from(k):
        slot = gate_in.at[line[k]]
        return remote(slot, slot, gs.at[k], gr.at[line[k]], sib)

    tab_from().wait_recv()
    for b in range(chips):
        own_keys(b).wait()
        key_from(b).wait_recv()
        value_from(b).wait_recv()

    def attend(b, side):
        query = qs[b, :, pl.ds(side * 2, 2)].reshape(CORES * 2 * rows, width)
        count = query.shape[0]
        lane = lax.broadcasted_iota(jnp.int32, (count, width), 1)
        in_head = [(lane >= j * head_dim) & (lane < (j + 1) * head_dim) for j in range(heads_here)]
        stack = jnp.concatenate(
            [query * jnp.where(at, 1.0, 0.0).astype(jnp.bfloat16) for at in in_head], axis=0
        )
        total = None
        for core in range(CORES):
            for t in range(slots):
                part = slice(t * tile, (t + 1) * tile)
                scores = lax.dot_general(
                    stack, keys[b, core, part], (((1,), (1,)), ((), ())),
                    preferred_element_type=jnp.float32,
                )
                bias = jnp.concatenate([tab[core, t, b]] * (tile // width), axis=1)
                half = jnp.concatenate(
                    [
                        scores[j * count : (j + 1) * count] + bias[j : j + 1]
                        for j in range(heads_here)
                    ],
                    axis=0,
                )
                weights = silu_of_half(half).astype(jnp.bfloat16)
                here = jnp.dot(weights, vals[b, core, part], preferred_element_type=jnp.float32)
                total = here if total is None else total + here
        result = total[:count]
        for j in range(1, heads_here):
            result = jnp.where(in_head[j], total[j * count : (j + 1) * count], result)
        return result.reshape(CORES, 2, rows, width).astype(jnp.bfloat16)

    def p_copy(b, zz, core):
        return remote(
            part_out.at[b, core, zz], part_in.at[h, b], ps.at[b], pr.at[h], zz * CORES + core
        )

    def step(k, carry):
        b = line_at(k)

        @pl.when(k == 0)
        def _():
            slot = qs.at[z, 1 - c]
            remote(slot, slot, qsem.at[0], qr.at[z], sib).wait_recv()

        @pl.when(k > 0)
        def _():
            remote(qs.at[b], qs.at[b], qsem.at[0], qr.at[b], sib).wait_recv()

        for side, group in ((1 - near, (3, 2)), (near, (1, 0))):
            part_out[b, :, pl.ds(side * 2, 2)] = attend(b, side)
            for i in group:
                if i > 0:
                    for core in range(CORES):
                        p_copy(b, line[i], core).start()
                else:
                    p_copy(b, z, 1 - c).start()
                    part_in[h, b] = part_out[b, c, z]

        @pl.when(k == 0)
        def _():
            w_gather(1)
            for j in range(n_cand):
                w_across(1, j).wait_recv()
            gate_out[...] = (
                silu_of_half(0.5 * jnp.dot(xn[...], wq[1], preferred_element_type=jnp.float32))
                .astype(jnp.bfloat16)
                .reshape(chips, rows, CORES * width)
            )
            for i in reversed(range(1, chips)):
                g_copy(i).start()
            gate_in[z] = gate_out[z]

        @pl.when((k == 1) & (inner == 0))
        def _():
            z_from(2).wait_recv()
            for j in range(1, n_cand):
                o_copy(j, 2).start()

        @pl.when((k == 1) & (inner == 0))
        def _():
            z_from(3).wait_recv()
            for j in range(1, n_cand):
                o_copy(j, 3).start()

        return carry

    z_from(1).wait_recv()
    for j in range(1, n_cand):
        o_copy(j, 1).start()

    @pl.when(inner == 1)
    def _():
        for k in (2, 3):
            z_from(k).wait_recv()
            z_onward(k).start()
            for j in range(1, n_cand):
                o_copy(j, k).start()

    lax.fori_loop(0, chips, step, 0)
    stage_in[3].wait()
    o_sib().start()
    for j in range(1, n_cand):
        for k in range(chips):
            o_copy(n_cand - j, k).wait_recv()
        c_copy(j).start()

    for k in range(1, chips):
        g_from(k).wait_recv()
    for i in range(1, n_hist):
        hh = lax.rem(h + i, n_hist)
        remote(part_in.at[hh], part_in.at[hh], ps.at[0], pr.at[hh], sib).wait_recv()
    columns = []
    gate_columns = []
    for hh in range(n_hist):
        b, core = hh // CORES, hh % CORES
        piece = part_in[core, b].astype(jnp.float32)
        for i in range(1, chips):
            piece = piece + part_in[i * CORES + core, b].astype(jnp.float32)
        columns.append(piece)
        gate_columns.append(gate_in[b, :, core * width : (core + 1) * width].astype(jnp.float32))
    attended = jnp.concatenate(columns, axis=1)
    gates = jnp.concatenate(gate_columns, axis=1)
    gated = (layer_norm(attended, out_gain_ref[...]) * gates).astype(jnp.bfloat16)
    sides = [
        jnp.concatenate(
            [gated[:, hh * width : (hh + 1) * width] for hh in range(side, n_hist, CORES)], axis=1
        )
        for side in range(CORES)
    ]
    wide = wo_ref.shape[1]
    o_sib().wait_recv()
    for j in range(1, n_cand):
        c_copy(j).wait_recv()
    for n in range(n_cand):
        part = slice(n * wide, (n + 1) * wide)
        total = inputs_ref[0, :, part].astype(jnp.float32)
        for side in range(CORES):
            total += jnp.dot(
                sides[side], wo[n, side].reshape(chips * width, wide),
                preferred_element_type=jnp.float32,
            )
        out_ref[0, :, part] = total.astype(jnp.bfloat16)
    tab_copy().wait_send()
    for k in range(chips):
        key_copy(k).wait_send()
        value_copy(k).wait_send()
        remote(q_out, q_out, qf.at[k], qr.at[z], sib).wait_send()
        for i in range(2):
            w_onward(i, k).wait_send()
        if k > 0:
            sent = qs.at[z, c]
            remote(sent, sent, qsem.at[k], qr.at[z], sib).wait_send()
            w_copy(0, k).wait_send()
            w_copy(1, k).wait_send()
            g_copy(k).wait_send()
    for k in (1, 2):
        z_copy(k).wait_send()
        x_copy(line[k]).wait_send()

    @pl.when(inner == 1)
    def _():
        for k in (2, 3):
            z_onward(k).wait_send()
            x_forward(k).wait_send()

    o_sib().wait_send()
    for j in range(1, n_cand):
        for k in range(chips):
            o_copy(j, k).wait_send()
        c_copy(j).wait_send()
    for k in range(chips):
        sent = part_in.at[pl.ds(0, n_hist - 1), 0]
        remote(sent, sent, ps.at[k], pr.at[0], sib).wait_send()


def fused_shards(
    n_cand, n_hist, inputs, in_gain, w_qu, out_gain, w_out, hist_keys, hist_values, pos_bias,
    lengths, tile_order, tile_mask,
):
    chips = n_hist // CORES
    rows, features = inputs.shape[1:]
    depth, width = w_qu.shape[1:]
    events = hist_keys.shape[1]
    slots = tile_order.shape[1]
    heads_here = width * pos_bias.shape[0] // features
    half, full = jnp.bfloat16, jnp.float32
    vmem = pl.BlockSpec(memory_space=pltpu.VMEM)
    hbm = pl.BlockSpec(memory_space=pltpu.HBM)
    dma = pltpu.SemaphoreType.DMA
    return pl.pallas_call(
        functools.partial(fused, n_cand, chips),
        out_shape=pltpu.VMEM(inputs.shape, half),
        in_specs=[hbm] * 11,
        out_specs=vmem,
        scratch_shapes=[
            pltpu.VMEM(inputs.shape, half),
            pltpu.VMEM((1, features), full),
            pltpu.VMEM((1, features), full),
            pltpu.SMEM(pos_bias.shape, full),
            pltpu.SMEM(lengths.shape, jnp.int32),
            pltpu.SMEM(tile_order.shape, jnp.int32),
            pltpu.SMEM(tile_mask.shape, jnp.int32),
            dma((9,)),
            pltpu.VMEM((chips * rows, features), half),
            pltpu.VMEM((2, depth * n_cand, CORES * width), half),
            pltpu.VMEM((n_cand, CORES, chips, width, w_out.shape[1]), half),
            pltpu.VMEM((chips, CORES, events, width), half),
            pltpu.VMEM((chips, CORES, events, width), half),
            pltpu.VMEM((chips, events, width), half),
            pltpu.VMEM((CORES, slots, chips, heads_here, width), full),
            pltpu.VMEM((slots, chips, heads_here, width), full),
            pltpu.VMEM((chips, CORES, chips, rows, width), half),
            pltpu.VMEM((chips, rows, width), half),
            pltpu.VMEM((chips, rows, CORES * width), half),
            pltpu.VMEM((chips, rows, CORES * width), half),
            pltpu.VMEM((chips, CORES, chips, rows, width), half),
            pltpu.VMEM((n_hist, chips, rows, width), half),
            dma((chips,)), dma((chips,)), dma((chips,)),
            dma((chips,)), dma((chips,)),
            dma((chips,)), dma((chips,)),
            dma((1,)), dma((1,)),
            dma((chips,)), dma((chips,)),
            dma((2, n_cand)), dma((2, n_cand)),
            dma((2, n_cand)), dma((2, n_cand)),
            dma((chips,)), dma((chips,)),
            dma((n_cand, chips)), dma((n_cand, chips)),
            dma((n_cand,)), dma((n_cand,)),
            dma((chips,)), dma((chips,)),
            dma((chips,)), dma((chips,)),
            dma((chips,)), dma((n_hist,)),
            dma((chips,)), dma((chips,)),
        ],
        compiler_params=pltpu.CompilerParams(
            collective_id=0, has_side_effects=True, vmem_limit_bytes=60 * 1024 * 1024
        ),
    )(
        inputs, in_gain[None], w_qu, out_gain[None], w_out, hist_keys, hist_values, pos_bias,
        lengths, tile_order, tile_mask,
    )


def solution(mesh):
    n_cand, n_hist = mesh.shape["cand"], mesh.shape["hist"]

    def local(*arrays):
        depth, width = arrays[2].shape[1:]
        head_dim = arrays[0].shape[2] // arrays[7].shape[0]
        fits = n_hist == 4 * CORES and width % 128 == 0 and width % head_dim == 0
        if fits and depth % 16 == 0 and arrays[0].shape[2] == width * n_hist:
            return fused_shards(n_cand, n_hist, *arrays)
        return shards(*arrays)

    placed = (
        P("cand", "hist", None),
        P(),
        P(None, "cand", "hist"),
        P(),
        P("hist", "cand"),
        P("cand", "hist", None),
        P("cand", "hist", None),
        P(),
        P("cand"),
        P("cand", "hist"),
        P("cand", "hist"),
    )
    return jax.shard_map(
        local, mesh=mesh, in_specs=placed, out_specs=P("cand", "hist", None), check_vma=False
    )
```

```python
import functools
import math

import jax
import jax.numpy as jnp
from jax import lax
from jax.experimental import pallas as pl
from jax.experimental.pallas import tpu as pltpu
from jax.sharding import PartitionSpec as P

EPS = 1e-05


def layer_norm(values, gain_vector):
    row_mean = jnp.mean(values, axis=-1, keepdims=True)
    square = jnp.mean(values * values, axis=-1, keepdims=True)
    return (values - row_mean) * lax.rsqrt(square - row_mean * row_mean + EPS) * gain_vector


def attention(all_queries, hist_keys, hist_values, pos_bias, lengths, tile_order, tile_mask):
    cands = all_queries.shape[1]
    width = all_queries.shape[2]
    heads = pos_bias.shape[0]
    tiles_all = pos_bias.shape[1]
    slots = tile_order.shape[1]
    tile = hist_keys.shape[1] // slots
    head_dim = width // heads
    score_scale = 1.0 / math.sqrt(head_dim)
    tile_numbers = jnp.arange(tiles_all, dtype=jnp.int32)
    offsets = jnp.arange(tile, dtype=jnp.int32)

    def one_user(user_items):
        user_query, key_block, value_block, slot_order, slot_mask, length = user_items
        query_heads = user_query.reshape(cands, heads, head_dim)
        one_hot = (slot_order[:, None] == tile_numbers[None, :]).astype(jnp.float32)
        slot_bias = jnp.dot(one_hot, pos_bias.T, precision=lax.Precision.HIGHEST)
        summed = jnp.zeros((cands, heads, head_dim), jnp.float32)
        for slot_index in range(slots):
            key_tile = key_block[slot_index * tile : (slot_index + 1) * tile].reshape(
                tile, heads, head_dim
            )
            value_tile = value_block[slot_index * tile : (slot_index + 1) * tile].reshape(
                tile, heads, head_dim
            )
            positions = slot_order[slot_index] * tile + offsets
            is_live = ((slot_mask[slot_index] == 1) & (positions < length)).astype(jnp.float32)
            bias_row = slot_bias[slot_index]

            def compute(
                key_tile=key_tile, value_tile=value_tile, is_live=is_live, bias_row=bias_row
            ):
                scores = jnp.einsum(
                    "chd,ehd->che", query_heads, key_tile, preferred_element_type=jnp.float32
                )
                scores = scores * score_scale + bias_row[None, :, None]
                weights = (jax.nn.silu(scores) * is_live[None, None, :]).astype(jnp.bfloat16)
                return jnp.einsum(
                    "che,ehd->chd", weights, value_tile, preferred_element_type=jnp.float32
                )

            summed = summed + compute()
        return summed.reshape(cands, width)

    return lax.map(one_user, (all_queries, hist_keys, hist_values, tile_order, tile_mask, lengths))


def shards(
    inputs,
    in_gain,
    w_qu,
    out_gain,
    w_out,
    hist_keys,
    hist_values,
    pos_bias,
    lengths,
    tile_order,
    tile_mask,
):
    w_full, out_rows = (
        lax.all_gather(w_qu, "cand", axis=1, tiled=True),
        lax.all_gather(w_out, "cand", axis=1, tiled=True),
    )
    normed = layer_norm(inputs.astype(jnp.float32), in_gain).astype(jnp.bfloat16)
    projected = jnp.einsum(
        "ucd,jdk->ucjk",
        normed,
        lax.all_gather(w_full, "hist", axis=2, tiled=True),
        preferred_element_type=jnp.float32,
    )
    queries = jax.nn.silu(projected[:, :, 0]).astype(jnp.bfloat16)
    gates = jax.nn.silu(projected[:, :, 1])
    all_queries = lax.all_gather(queries, "hist", axis=1, tiled=True)
    attended = attention(
        all_queries, hist_keys, hist_values, pos_bias, lengths, tile_order, tile_mask
    )
    own_rows = lax.psum_scatter(
        attended.astype(jnp.bfloat16), "hist", scatter_dimension=1, tiled=True
    ).astype(jnp.float32)
    gated = (layer_norm(own_rows, out_gain) * gates).astype(jnp.bfloat16)
    projected_out = jnp.einsum(
        "uck,kd->ucd",
        gated,
        lax.all_gather(out_rows, "hist", axis=0, tiled=True),
        preferred_element_type=jnp.float32,
    )
    return (inputs.astype(jnp.float32) + projected_out).astype(jnp.bfloat16)


MESH = pl.DeviceIdType.MESH
CORES = 2


def silu_of_half(half):
    return half + half * jnp.tanh(half)


def fused(
    n_cand, chips, inputs_hbm, in_gain_hbm, w_ref, out_gain_hbm, wo_ref, k_hbm, v_hbm, bias_hbm,
    len_hbm, order_hbm, mask_hbm, out_ref,
    inputs_ref, in_gain_ref, out_gain_ref, bias_ref, len_ref, order_ref, mask_ref, in_sem, xn,
    wq, wo, keys, vals, vals_out, tab, tab_out, qs, q_out, gate_out, gate_in, part_out, part_in,
    k_own, v_own, v_other, ks, kr, vs, vr, ts, tr, xs, xr, fs, fr, ws, wr, zs, zr, os, orr, cs, cr,
    gs, gr, qsem, qr, ps, pr, xf, qf,
):
    n_hist = chips * CORES
    u = lax.axis_index("cand")
    h = lax.axis_index("hist")
    z = lax.div(h, CORES)
    c = lax.rem(h, CORES)
    sib = z * CORES + (1 - c)
    rows = inputs_hbm.shape[1]
    width = w_ref.shape[2]
    depth = w_ref.shape[1]
    features = inputs_hbm.shape[2]
    slots = order_ref.shape[1]
    events = k_hbm.shape[1]
    tile = events // slots
    pair = CORES * rows
    heads_here = width * bias_ref.shape[0] // features
    head_dim = width // heads_here

    inner = lax.rem(lax.div(z + 1, 2), 2)
    across = lax.rem(z + 2, chips)
    mirror = chips - 1 - z
    line = [
        z,
        z + 1 - 2 * lax.rem(z, 2),
        inner * mirror + (1 - inner) * across,
        inner * across + (1 - inner) * mirror,
    ]

    def line_at(k):
        place = line[chips - 1]
        for i in range(chips - 1):
            place = jnp.where(k == i, line[i], place)
        return place

    def chip_at(k):
        return lax.rem(z + k, chips)

    def remote(src, dst, send, recv, hist_to, cand_to=None):
        return pltpu.make_async_remote_copy(
            src_ref=src, dst_ref=dst, send_sem=send, recv_sem=recv,
            device_id=(u if cand_to is None else cand_to, hist_to), device_id_type=MESH,
        )

    mine = pl.ds(pl.multiple_of(c * width, width), width)
    theirs = pl.ds(pl.multiple_of((1 - c) * width, width), width)
    stage_in = [
        pltpu.make_async_copy(src, dst, in_sem.at[i])
        for i, (src, dst) in enumerate(
            (
                (inputs_hbm, inputs_ref),
                (in_gain_hbm, in_gain_ref),
                (w_ref, wq.at[:, pl.ds(pl.multiple_of(u * depth, depth), depth), mine]),
                (wo_ref, wo.at[u, c, z]),
                (out_gain_hbm, out_gain_ref),
                (bias_hbm, bias_ref),
                (len_hbm, len_ref),
                (order_hbm, order_ref),
                (mask_hbm, mask_ref),
            )
        )
    ]
    stage_in[0].start()
    stage_in[1].start()
    barrier = pltpu.get_barrier_semaphore()
    for i in range(1, n_hist):
        pl.semaphore_signal(
            barrier, inc=1, device_id=(u, lax.rem(h + i, n_hist)), device_id_type=MESH
        )
    for j in range(1, n_cand):
        pl.semaphore_signal(
            barrier, inc=1, device_id=(lax.rem(u + j, n_cand), h), device_id_type=MESH
        )
    for copy in stage_in[2:]:
        copy.start()

    def columns_of(ref, b, core):
        return ref.at[0, :, pl.ds(pl.multiple_of((b * CORES + core) * width, width), width)]

    def own_keys(b):
        return pltpu.make_async_copy(columns_of(k_hbm, b, c), keys.at[b, c], k_own.at[b])

    def own_values(b):
        return pltpu.make_async_copy(columns_of(v_hbm, b, c), vals.at[b, c], v_own.at[b])

    def other_values(b):
        return pltpu.make_async_copy(columns_of(v_hbm, b, 1 - c), vals_out.at[b], v_other.at[b])

    for b in range(chips):
        other_values(b).start()
    for b in range(chips):
        own_values(b).start()
        own_keys(b).start()

    stage_in[0].wait()
    stage_in[1].wait()
    normed = layer_norm(inputs_ref[0].astype(jnp.float32), in_gain_ref[...])

    def x_at(zz):
        return xn.at[pl.ds(pl.multiple_of(zz * rows, rows), rows)]

    x_at(z)[...] = normed.astype(jnp.bfloat16)
    pl.semaphore_wait(barrier, n_hist - 1 + n_cand - 1)

    def w_slot(i, uu):
        return wq.at[i, pl.ds(pl.multiple_of(uu * depth, depth), depth), mine]

    def w_copy(i, j):
        return remote(
            w_ref.at[i], w_slot(i, u), ws.at[i, j], wr.at[i, n_cand - j], h, lax.rem(u + j, n_cand)
        )

    def w_onward(i, j):
        slot = w_slot(i, lax.rem(u + j, n_cand))
        return remote(slot, slot, fs.at[i, j], fr.at[i, j], sib)

    def w_across(i, j):
        uu = lax.rem(u + j, n_cand)
        slot = wq.at[i, pl.ds(pl.multiple_of(uu * depth, depth), depth), theirs]
        return remote(slot, slot, fs.at[i, j], fr.at[i, j], sib)

    def w_gather(i):
        for j in range(1, n_cand):
            w_copy(i, n_cand - j).wait_recv()
            w_onward(i, j).start()

    def z_copy(k):
        return remote(wo_ref, wo.at[u, c, z], zs.at[k], zr.at[z], line[k] * CORES + c)

    def z_from(k):
        slot = wo.at[u, c, line[k]]
        return remote(slot, slot, zs.at[k], zr.at[line[k]], sib)

    def z_onward(k):
        slot = wo.at[u, c, line[k]]
        return remote(slot, slot, zs.at[3 * (k - 2)], zr.at[line[k]], line[1] * CORES + c)

    def o_sib():
        return remote(wo.at[u, c], wo.at[u, c], os.at[0, 0], orr.at[0, 0], sib)

    def o_copy(j, k):
        slot = wo.at[u, c, line[k]]
        return remote(
            wo_ref if k == 0 else slot, slot, os.at[j, k], orr.at[n_cand - j, k], h,
            lax.rem(u + j, n_cand),
        )

    def c_copy(j):
        uu = lax.rem(u + j, n_cand)
        return remote(wo.at[uu, c], wo.at[uu, c], cs.at[j], cr.at[j], sib)

    def x_copy(zz):
        return remote(x_at(z), x_at(z), xs.at[zz], xr.at[z], zz * CORES + c)

    def x_from(zz):
        return remote(x_at(zz), x_at(zz), xs.at[zz], xr.at[zz], sib)

    def x_forward(k):
        return remote(
            x_at(line[k]), x_at(line[k]), xf.at[k], xr.at[line[k]], line[1] * CORES + c
        )

    def key_copy(b):
        return remote(columns_of(k_hbm, b, 1 - c), keys.at[b, c], ks.at[b], kr.at[b], sib)

    def value_copy(b):
        return remote(vals_out.at[b], vals.at[b, c], vs.at[b], vr.at[b], sib)

    def key_from(b):
        return remote(keys.at[b, 1 - c], keys.at[b, 1 - c], ks.at[b], kr.at[b], sib)

    def value_from(b):
        return remote(vals.at[b, 1 - c], vals.at[b, 1 - c], vs.at[b], vr.at[b], sib)

    def tab_copy():
        return remote(tab_out, tab.at[c], ts.at[0], tr.at[0], sib)

    def tab_from():
        return remote(tab_out, tab.at[1 - c], ts.at[0], tr.at[0], sib)

    for j in range(1, n_cand):
        w_copy(0, j).start()
    for k in (2, 1):
        x_copy(line[k]).start()
    z_copy(1).start()
    z_copy(2).start()
    for j in range(1, n_cand):
        o_copy(j, 0).start()
    for j in range(1, n_cand):
        w_copy(1, j).start()
    stage_in[2].wait()
    w_onward(0, 0).start()
    w_onward(1, 0).start()
    for b in range(chips):
        key_copy(b).start()

    for copy in stage_in[4:]:
        copy.wait()
    for t in range(slots):
        for b in range(chips):
            for j in range(heads_here):
                for core in range(CORES):
                    head = (b * CORES + core) * heads_here + j
                    row = jnp.full((1, width), 0.5 * bias_ref[head, order_ref[0, t]], jnp.float32)
                    is_own = c == core

                    @pl.when(is_own)
                    def _(t=t, b=b, j=j, row=row):
                        tab[c, t, b, j : j + 1] = row

                    @pl.when(jnp.logical_not(is_own))
                    def _(t=t, b=b, j=j, row=row):
                        tab_out[t, b, j : j + 1] = row
    tab_copy().start()
    live = []
    for t in range(slots):
        limit = jnp.where(mask_ref[0, t] == 1, len_ref[0] - order_ref[0, t] * tile, 0)
        place = lax.broadcasted_iota(jnp.int32, (tile, width), 0)
        live.append(jnp.where(place < limit, 1.0, 0.0).astype(jnp.bfloat16))
    for b in range(chips):
        other_values(b).wait()
        for t in range(slots):
            part = slice(t * tile, (t + 1) * tile)
            vals_out[b, part] = vals_out[b, part] * live[t]
        value_copy(b).start()
    for b in range(chips):
        own_values(b).wait()
        for t in range(slots):
            part = slice(t * tile, (t + 1) * tile)
            vals[b, c, part] = vals[b, c, part] * live[t]

    @pl.when(inner == 1)
    def _():
        for k in (2, 3):
            x_from(line[k]).wait_recv()
            x_forward(k).start()

    w_gather(0)
    score_scale = 0.5 / math.sqrt(head_dim)
    near = lax.div(z, 2)

    def half_at(b, core, side):
        return qs.at[b, core, pl.ds(side * 2, 2)]

    def q_out_at(side):
        return q_out.at[pl.ds(side * 2, 2)]

    def q_copy(side, k):
        piece = half_at(z, c, side)
        return remote(piece, piece, qsem.at[k], qr.at[z], line[k] * CORES + c)

    def q_cross(side, k):
        return remote(
            q_out_at(side), half_at(z, c, side), qf.at[k], qr.at[z], line[k] * CORES + (1 - c)
        )

    def query(side):
        block = xn[pl.ds(pl.multiple_of(side * pair, pair), pair)]
        half_query = 0.5 * jnp.dot(block, wq[0], preferred_element_type=jnp.float32)
        made = (silu_of_half(half_query) * score_scale).astype(jnp.bfloat16)
        parts = [
            made[:, core * width : (core + 1) * width].reshape(2, rows, width)
            for core in range(CORES)
        ]
        half_at(z, c, side)[...] = jnp.where(c == 0, parts[0], parts[1])
        q_out_at(side)[...] = jnp.where(c == 0, parts[1], parts[0])
        for k in reversed(range(1, chips)):
            q_copy(side, k).start()
            q_cross(side, k).start()
        q_cross(side, 0).start()

    @pl.when(inner == 1)
    def _():
        z_from(2).wait_recv()
        z_onward(2).start()

    for j in range(n_cand):
        w_across(0, j).wait_recv()
    x_from(line[1]).wait_recv()
    query(near)

    @pl.when(inner == 0)
    def _():
        for k in (2, 3):
            x_from(line[k]).wait_recv()

    query(1 - near)

    def g_copy(k):
        return remote(gate_out.at[line[k]], gate_in.at[z], gs.at[k], gr.at[z], line[k] * CORES + c)

    def g_from(k):
        slot = gate_in.at[line[k]]
        return remote(slot, slot, gs.at[k], gr.at[line[k]], sib)

    tab_from().wait_recv()
    for b in range(chips):
        own_keys(b).wait()
        key_from(b).wait_recv()
        value_from(b).wait_recv()

    def attend(b, side):
        query = qs[b, :, pl.ds(side * 2, 2)].reshape(CORES * 2 * rows, width)
        count = query.shape[0]
        lane = lax.broadcasted_iota(jnp.int32, (count, width), 1)
        in_head = [(lane >= j * head_dim) & (lane < (j + 1) * head_dim) for j in range(heads_here)]
        stack = jnp.concatenate(
            [query * jnp.where(at, 1.0, 0.0).astype(jnp.bfloat16) for at in in_head], axis=0
        )
        total = None
        for core in range(CORES):
            for t in range(slots):
                part = slice(t * tile, (t + 1) * tile)
                scores = lax.dot_general(
                    stack, keys[b, core, part], (((1,), (1,)), ((), ())),
                    preferred_element_type=jnp.float32,
                )
                bias = jnp.concatenate([tab[core, t, b]] * (tile // width), axis=1)
                half = jnp.concatenate(
                    [
                        scores[j * count : (j + 1) * count] + bias[j : j + 1]
                        for j in range(heads_here)
                    ],
                    axis=0,
                )
                weights = silu_of_half(half).astype(jnp.bfloat16)
                here = jnp.dot(weights, vals[b, core, part], preferred_element_type=jnp.float32)
                total = here if total is None else total + here
        result = total[:count]
        for j in range(1, heads_here):
            result = jnp.where(in_head[j], total[j * count : (j + 1) * count], result)
        return result.reshape(CORES, 2, rows, width).astype(jnp.bfloat16)

    def p_copy(b, zz, core):
        return remote(
            part_out.at[b, core, zz], part_in.at[h, b], ps.at[b], pr.at[h], zz * CORES + core
        )

    def step(k, carry):
        b = line_at(k)

        @pl.when(k == 0)
        def _():
            slot = qs.at[z, 1 - c]
            remote(slot, slot, qsem.at[0], qr.at[z], sib).wait_recv()

        @pl.when(k > 0)
        def _():
            remote(qs.at[b], qs.at[b], qsem.at[0], qr.at[b], sib).wait_recv()

        for side, group in ((1 - near, (3, 2)), (near, (1, 0))):
            part_out[b, :, pl.ds(side * 2, 2)] = attend(b, side)
            for i in group:
                if i > 0:
                    for core in range(CORES):
                        p_copy(b, line[i], core).start()
                else:
                    p_copy(b, z, 1 - c).start()
                    part_in[h, b] = part_out[b, c, z]

        @pl.when(k == 0)
        def _():
            w_gather(1)
            for j in range(n_cand):
                w_across(1, j).wait_recv()
            gate_out[...] = (
                silu_of_half(0.5 * jnp.dot(xn[...], wq[1], preferred_element_type=jnp.float32))
                .astype(jnp.bfloat16)
                .reshape(chips, rows, CORES * width)
            )
            for i in reversed(range(1, chips)):
                g_copy(i).start()
            gate_in[z] = gate_out[z]

        @pl.when((k == 0) & (inner == 0))
        def _():
            z_from(2).wait_recv()
            for j in range(1, n_cand):
                o_copy(j, 2).start()

        @pl.when((k == 1) & (inner == 0))
        def _():
            z_from(3).wait_recv()
            for j in range(1, n_cand):
                o_copy(j, 3).start()

        return carry

    z_from(1).wait_recv()
    for j in range(1, n_cand):
        o_copy(j, 1).start()

    @pl.when(inner == 1)
    def _():
        for j in range(1, n_cand):
            o_copy(j, 2).start()

    @pl.when(inner == 1)
    def _():
        z_from(3).wait_recv()
        z_onward(3).start()
        for j in range(1, n_cand):
            o_copy(j, 3).start()

    lax.fori_loop(0, chips, step, 0)
    stage_in[3].wait()
    o_sib().start()
    for j in range(1, n_cand):
        for k in range(chips):
            o_copy(n_cand - j, k).wait_recv()
        c_copy(j).start()

    for k in range(1, chips):
        g_from(k).wait_recv()
    for i in range(1, n_hist):
        hh = lax.rem(h + i, n_hist)
        remote(part_in.at[hh], part_in.at[hh], ps.at[0], pr.at[hh], sib).wait_recv()
    columns = []
    gate_columns = []
    for hh in range(n_hist):
        b, core = hh // CORES, hh % CORES
        piece = part_in[core, b].astype(jnp.float32)
        for i in range(1, chips):
            piece = piece + part_in[i * CORES + core, b].astype(jnp.float32)
        columns.append(piece)
        gate_columns.append(gate_in[b, :, core * width : (core + 1) * width].astype(jnp.float32))
    attended = jnp.concatenate(columns, axis=1)
    gates = jnp.concatenate(gate_columns, axis=1)
    gated = (layer_norm(attended, out_gain_ref[...]) * gates).astype(jnp.bfloat16)
    sides = [
        jnp.concatenate(
            [gated[:, hh * width : (hh + 1) * width] for hh in range(side, n_hist, CORES)], axis=1
        )
        for side in range(CORES)
    ]
    wide = wo_ref.shape[1]
    o_sib().wait_recv()
    for j in range(1, n_cand):
        c_copy(j).wait_recv()
    for n in range(n_cand):
        part = slice(n * wide, (n + 1) * wide)
        total = inputs_ref[0, :, part].astype(jnp.float32)
        for side in range(CORES):
            total += jnp.dot(
                sides[side], wo[n, side].reshape(chips * width, wide),
                preferred_element_type=jnp.float32,
            )
        out_ref[0, :, part] = total.astype(jnp.bfloat16)
    tab_copy().wait_send()
    for k in range(chips):
        key_copy(k).wait_send()
        value_copy(k).wait_send()
        remote(q_out, q_out, qf.at[k], qr.at[z], sib).wait_send()
        for i in range(2):
            w_onward(i, k).wait_send()
        if k > 0:
            sent = qs.at[z, c]
            remote(sent, sent, qsem.at[k], qr.at[z], sib).wait_send()
            w_copy(0, k).wait_send()
            w_copy(1, k).wait_send()
            g_copy(k).wait_send()
    for k in (1, 2):
        z_copy(k).wait_send()
        x_copy(line[k]).wait_send()

    @pl.when(inner == 1)
    def _():
        for k in (2, 3):
            z_onward(k).wait_send()
            x_forward(k).wait_send()

    o_sib().wait_send()
    for j in range(1, n_cand):
        for k in range(chips):
            o_copy(j, k).wait_send()
        c_copy(j).wait_send()
    for k in range(chips):
        sent = part_in.at[pl.ds(0, n_hist - 1), 0]
        remote(sent, sent, ps.at[k], pr.at[0], sib).wait_send()


def fused_shards(
    n_cand, n_hist, inputs, in_gain, w_qu, out_gain, w_out, hist_keys, hist_values, pos_bias,
    lengths, tile_order, tile_mask,
):
    chips = n_hist // CORES
    rows, features = inputs.shape[1:]
    depth, width = w_qu.shape[1:]
    events = hist_keys.shape[1]
    slots = tile_order.shape[1]
    heads_here = width * pos_bias.shape[0] // features
    half, full = jnp.bfloat16, jnp.float32
    vmem = pl.BlockSpec(memory_space=pltpu.VMEM)
    hbm = pl.BlockSpec(memory_space=pltpu.HBM)
    dma = pltpu.SemaphoreType.DMA
    return pl.pallas_call(
        functools.partial(fused, n_cand, chips),
        out_shape=pltpu.VMEM(inputs.shape, half),
        in_specs=[hbm] * 11,
        out_specs=vmem,
        scratch_shapes=[
            pltpu.VMEM(inputs.shape, half),
            pltpu.VMEM((1, features), full),
            pltpu.VMEM((1, features), full),
            pltpu.SMEM(pos_bias.shape, full),
            pltpu.SMEM(lengths.shape, jnp.int32),
            pltpu.SMEM(tile_order.shape, jnp.int32),
            pltpu.SMEM(tile_mask.shape, jnp.int32),
            dma((9,)),
            pltpu.VMEM((chips * rows, features), half),
            pltpu.VMEM((2, depth * n_cand, CORES * width), half),
            pltpu.VMEM((n_cand, CORES, chips, width, w_out.shape[1]), half),
            pltpu.VMEM((chips, CORES, events, width), half),
            pltpu.VMEM((chips, CORES, events, width), half),
            pltpu.VMEM((chips, events, width), half),
            pltpu.VMEM((CORES, slots, chips, heads_here, width), full),
            pltpu.VMEM((slots, chips, heads_here, width), full),
            pltpu.VMEM((chips, CORES, chips, rows, width), half),
            pltpu.VMEM((chips, rows, width), half),
            pltpu.VMEM((chips, rows, CORES * width), half),
            pltpu.VMEM((chips, rows, CORES * width), half),
            pltpu.VMEM((chips, CORES, chips, rows, width), half),
            pltpu.VMEM((n_hist, chips, rows, width), half),
            dma((chips,)), dma((chips,)), dma((chips,)),
            dma((chips,)), dma((chips,)),
            dma((chips,)), dma((chips,)),
            dma((1,)), dma((1,)),
            dma((chips,)), dma((chips,)),
            dma((2, n_cand)), dma((2, n_cand)),
            dma((2, n_cand)), dma((2, n_cand)),
            dma((chips,)), dma((chips,)),
            dma((n_cand, chips)), dma((n_cand, chips)),
            dma((n_cand,)), dma((n_cand,)),
            dma((chips,)), dma((chips,)),
            dma((chips,)), dma((chips,)),
            dma((chips,)), dma((n_hist,)),
            dma((chips,)), dma((chips,)),
        ],
        compiler_params=pltpu.CompilerParams(
            collective_id=0, has_side_effects=True, vmem_limit_bytes=60 * 1024 * 1024
        ),
    )(
        inputs, in_gain[None], w_qu, out_gain[None], w_out, hist_keys, hist_values, pos_bias,
        lengths, tile_order, tile_mask,
    )


def solution(mesh):
    n_cand, n_hist = mesh.shape["cand"], mesh.shape["hist"]

    def local(*arrays):
        depth, width = arrays[2].shape[1:]
        head_dim = arrays[0].shape[2] // arrays[7].shape[0]
        fits = n_hist == 4 * CORES and width % 128 == 0 and width % head_dim == 0
        if fits and depth % 16 == 0 and arrays[0].shape[2] == width * n_hist:
            return fused_shards(n_cand, n_hist, *arrays)
        return shards(*arrays)

    placed = (
        P("cand", "hist", None),
        P(),
        P(None, "cand", "hist"),
        P(),
        P("hist", "cand"),
        P("cand", "hist", None),
        P("cand", "hist", None),
        P(),
        P("cand"),
        P("cand", "hist"),
        P("cand", "hist"),
    )
    return jax.shard_map(
        local, mesh=mesh, in_specs=placed, out_specs=P("cand", "hist", None), check_vma=False
    )
```

```python
import functools
import math

import jax
import jax.numpy as jnp
from jax import lax
from jax.experimental import pallas as pl
from jax.experimental.pallas import tpu as pltpu
from jax.sharding import PartitionSpec as P

EPS = 1e-05


def layer_norm(values, gain_vector):
    row_mean = jnp.mean(values, axis=-1, keepdims=True)
    square = jnp.mean(values * values, axis=-1, keepdims=True)
    return (values - row_mean) * lax.rsqrt(square - row_mean * row_mean + EPS) * gain_vector


def attention(all_queries, hist_keys, hist_values, pos_bias, lengths, tile_order, tile_mask):
    cands = all_queries.shape[1]
    width = all_queries.shape[2]
    heads = pos_bias.shape[0]
    tiles_all = pos_bias.shape[1]
    slots = tile_order.shape[1]
    tile = hist_keys.shape[1] // slots
    head_dim = width // heads
    score_scale = 1.0 / math.sqrt(head_dim)
    tile_numbers = jnp.arange(tiles_all, dtype=jnp.int32)
    offsets = jnp.arange(tile, dtype=jnp.int32)

    def one_user(user_items):
        user_query, key_block, value_block, slot_order, slot_mask, length = user_items
        query_heads = user_query.reshape(cands, heads, head_dim)
        one_hot = (slot_order[:, None] == tile_numbers[None, :]).astype(jnp.float32)
        slot_bias = jnp.dot(one_hot, pos_bias.T, precision=lax.Precision.HIGHEST)
        summed = jnp.zeros((cands, heads, head_dim), jnp.float32)
        for slot_index in range(slots):
            key_tile = key_block[slot_index * tile : (slot_index + 1) * tile].reshape(
                tile, heads, head_dim
            )
            value_tile = value_block[slot_index * tile : (slot_index + 1) * tile].reshape(
                tile, heads, head_dim
            )
            positions = slot_order[slot_index] * tile + offsets
            is_live = ((slot_mask[slot_index] == 1) & (positions < length)).astype(jnp.float32)
            bias_row = slot_bias[slot_index]

            def compute(
                key_tile=key_tile, value_tile=value_tile, is_live=is_live, bias_row=bias_row
            ):
                scores = jnp.einsum(
                    "chd,ehd->che", query_heads, key_tile, preferred_element_type=jnp.float32
                )
                scores = scores * score_scale + bias_row[None, :, None]
                weights = (jax.nn.silu(scores) * is_live[None, None, :]).astype(jnp.bfloat16)
                return jnp.einsum(
                    "che,ehd->chd", weights, value_tile, preferred_element_type=jnp.float32
                )

            summed = summed + compute()
        return summed.reshape(cands, width)

    return lax.map(one_user, (all_queries, hist_keys, hist_values, tile_order, tile_mask, lengths))


def shards(
    inputs,
    in_gain,
    w_qu,
    out_gain,
    w_out,
    hist_keys,
    hist_values,
    pos_bias,
    lengths,
    tile_order,
    tile_mask,
):
    w_full, out_rows = (
        lax.all_gather(w_qu, "cand", axis=1, tiled=True),
        lax.all_gather(w_out, "cand", axis=1, tiled=True),
    )
    normed = layer_norm(inputs.astype(jnp.float32), in_gain).astype(jnp.bfloat16)
    projected = jnp.einsum(
        "ucd,jdk->ucjk",
        normed,
        lax.all_gather(w_full, "hist", axis=2, tiled=True),
        preferred_element_type=jnp.float32,
    )
    queries = jax.nn.silu(projected[:, :, 0]).astype(jnp.bfloat16)
    gates = jax.nn.silu(projected[:, :, 1])
    all_queries = lax.all_gather(queries, "hist", axis=1, tiled=True)
    attended = attention(
        all_queries, hist_keys, hist_values, pos_bias, lengths, tile_order, tile_mask
    )
    own_rows = lax.psum_scatter(
        attended.astype(jnp.bfloat16), "hist", scatter_dimension=1, tiled=True
    ).astype(jnp.float32)
    gated = (layer_norm(own_rows, out_gain) * gates).astype(jnp.bfloat16)
    projected_out = jnp.einsum(
        "uck,kd->ucd",
        gated,
        lax.all_gather(out_rows, "hist", axis=0, tiled=True),
        preferred_element_type=jnp.float32,
    )
    return (inputs.astype(jnp.float32) + projected_out).astype(jnp.bfloat16)


MESH = pl.DeviceIdType.MESH
CORES = 2


def silu_of_half(half):
    return half + half * jnp.tanh(half)


def fused(
    n_cand, chips, inputs_hbm, in_gain_hbm, w_ref, out_gain_hbm, wo_ref, k_hbm, v_hbm, bias_hbm,
    len_hbm, order_hbm, mask_hbm, out_ref,
    inputs_ref, in_gain_ref, out_gain_ref, bias_ref, len_ref, order_ref, mask_ref, in_sem, xn,
    wq, wo, keys, vals, vals_out, tab, tab_out, qs, q_out, gate_out, gate_in, part_out, part_in,
    k_own, v_own, v_other, ks, kr, vs, vr, ts, tr, xs, xr, fs, fr, ws, wr, zs, zr, os, orr, cs, cr,
    gs, gr, qsem, qr, ps, pr, xf, qf,
):
    n_hist = chips * CORES
    u = lax.axis_index("cand")
    h = lax.axis_index("hist")
    z = lax.div(h, CORES)
    c = lax.rem(h, CORES)
    sib = z * CORES + (1 - c)
    rows = inputs_hbm.shape[1]
    width = w_ref.shape[2]
    depth = w_ref.shape[1]
    features = inputs_hbm.shape[2]
    slots = order_ref.shape[1]
    events = k_hbm.shape[1]
    tile = events // slots
    pair = CORES * rows
    heads_here = width * bias_ref.shape[0] // features
    head_dim = width // heads_here

    inner = lax.rem(lax.div(z + 1, 2), 2)
    across = lax.rem(z + 2, chips)
    mirror = chips - 1 - z
    line = [
        z,
        z + 1 - 2 * lax.rem(z, 2),
        inner * mirror + (1 - inner) * across,
        inner * across + (1 - inner) * mirror,
    ]

    def line_at(k):
        place = line[chips - 1]
        for i in range(chips - 1):
            place = jnp.where(k == i, line[i], place)
        return place

    def chip_at(k):
        return lax.rem(z + k, chips)

    def remote(src, dst, send, recv, hist_to, cand_to=None):
        return pltpu.make_async_remote_copy(
            src_ref=src, dst_ref=dst, send_sem=send, recv_sem=recv,
            device_id=(u if cand_to is None else cand_to, hist_to), device_id_type=MESH,
        )

    mine = pl.ds(pl.multiple_of(c * width, width), width)
    theirs = pl.ds(pl.multiple_of((1 - c) * width, width), width)
    stage_in = [
        pltpu.make_async_copy(src, dst, in_sem.at[i])
        for i, (src, dst) in enumerate(
            (
                (inputs_hbm, inputs_ref),
                (in_gain_hbm, in_gain_ref),
                (w_ref, wq.at[:, pl.ds(pl.multiple_of(u * depth, depth), depth), mine]),
                (wo_ref, wo.at[u, c, z]),
                (out_gain_hbm, out_gain_ref),
                (bias_hbm, bias_ref),
                (len_hbm, len_ref),
                (order_hbm, order_ref),
                (mask_hbm, mask_ref),
            )
        )
    ]
    stage_in[0].start()
    stage_in[1].start()
    barrier = pltpu.get_barrier_semaphore()
    for i in range(1, n_hist):
        pl.semaphore_signal(
            barrier, inc=1, device_id=(u, lax.rem(h + i, n_hist)), device_id_type=MESH
        )
    for j in range(1, n_cand):
        pl.semaphore_signal(
            barrier, inc=1, device_id=(lax.rem(u + j, n_cand), h), device_id_type=MESH
        )
    for copy in stage_in[2:]:
        copy.start()

    def columns_of(ref, b, core):
        return ref.at[0, :, pl.ds(pl.multiple_of((b * CORES + core) * width, width), width)]

    def own_keys(b):
        return pltpu.make_async_copy(columns_of(k_hbm, b, c), keys.at[b, c], k_own.at[b])

    def own_values(b):
        return pltpu.make_async_copy(columns_of(v_hbm, b, c), vals.at[b, c], v_own.at[b])

    def other_values(b):
        return pltpu.make_async_copy(columns_of(v_hbm, b, 1 - c), vals_out.at[b], v_other.at[b])

    for b in range(chips):
        other_values(b).start()
    for b in range(chips):
        own_values(b).start()
        own_keys(b).start()

    stage_in[0].wait()
    stage_in[1].wait()
    normed = layer_norm(inputs_ref[0].astype(jnp.float32), in_gain_ref[...])

    def x_at(zz):
        return xn.at[pl.ds(pl.multiple_of(zz * rows, rows), rows)]

    x_at(z)[...] = normed.astype(jnp.bfloat16)
    pl.semaphore_wait(barrier, n_hist - 1 + n_cand - 1)

    def w_slot(i, uu):
        return wq.at[i, pl.ds(pl.multiple_of(uu * depth, depth), depth), mine]

    def w_copy(i, j):
        return remote(
            w_ref.at[i], w_slot(i, u), ws.at[i, j], wr.at[i, n_cand - j], h, lax.rem(u + j, n_cand)
        )

    def w_onward(i, j):
        slot = w_slot(i, lax.rem(u + j, n_cand))
        return remote(slot, slot, fs.at[i, j], fr.at[i, j], sib)

    def w_across(i, j):
        uu = lax.rem(u + j, n_cand)
        slot = wq.at[i, pl.ds(pl.multiple_of(uu * depth, depth), depth), theirs]
        return remote(slot, slot, fs.at[i, j], fr.at[i, j], sib)

    def w_gather(i):
        for j in range(1, n_cand):
            w_copy(i, n_cand - j).wait_recv()
            w_onward(i, j).start()

    def z_copy(k):
        return remote(wo_ref, wo.at[u, c, z], zs.at[k], zr.at[z], line[k] * CORES + c)

    def z_from(k):
        slot = wo.at[u, c, line[k]]
        return remote(slot, slot, zs.at[k], zr.at[line[k]], sib)

    def z_onward(k):
        slot = wo.at[u, c, line[k]]
        return remote(slot, slot, zs.at[3 * (k - 2)], zr.at[line[k]], line[1] * CORES + c)

    def o_sib():
        return remote(wo.at[u, c], wo.at[u, c], os.at[0, 0], orr.at[0, 0], sib)

    def o_copy(j, k):
        slot = wo.at[u, c, line[k]]
        return remote(
            wo_ref if k == 0 else slot, slot, os.at[j, k], orr.at[n_cand - j, k], h,
            lax.rem(u + j, n_cand),
        )

    def c_copy(j):
        uu = lax.rem(u + j, n_cand)
        return remote(wo.at[uu, c], wo.at[uu, c], cs.at[j], cr.at[j], sib)

    def x_copy(zz):
        return remote(x_at(z), x_at(z), xs.at[zz], xr.at[z], zz * CORES + c)

    def x_from(zz):
        return remote(x_at(zz), x_at(zz), xs.at[zz], xr.at[zz], sib)

    def x_forward(k):
        return remote(
            x_at(line[k]), x_at(line[k]), xf.at[k], xr.at[line[k]], line[1] * CORES + c
        )

    def key_copy(b):
        return remote(columns_of(k_hbm, b, 1 - c), keys.at[b, c], ks.at[b], kr.at[b], sib)

    def value_copy(b):
        return remote(vals_out.at[b], vals.at[b, c], vs.at[b], vr.at[b], sib)

    def key_from(b):
        return remote(keys.at[b, 1 - c], keys.at[b, 1 - c], ks.at[b], kr.at[b], sib)

    def value_from(b):
        return remote(vals.at[b, 1 - c], vals.at[b, 1 - c], vs.at[b], vr.at[b], sib)

    def tab_copy():
        return remote(tab_out, tab.at[c], ts.at[0], tr.at[0], sib)

    def tab_from():
        return remote(tab_out, tab.at[1 - c], ts.at[0], tr.at[0], sib)

    for j in range(1, n_cand):
        w_copy(0, j).start()
    for k in (2, 1):
        x_copy(line[k]).start()
    z_copy(1).start()
    z_copy(2).start()
    for j in range(1, n_cand):
        o_copy(j, 0).start()
    for j in range(1, n_cand):
        w_copy(1, j).start()
    stage_in[2].wait()
    w_onward(0, 0).start()
    w_onward(1, 0).start()
    for b in range(chips):
        key_copy(b).start()

    for copy in stage_in[4:]:
        copy.wait()
    for t in range(slots):
        for b in range(chips):
            for j in range(heads_here):
                for core in range(CORES):
                    head = (b * CORES + core) * heads_here + j
                    row = jnp.full((1, width), 0.5 * bias_ref[head, order_ref[0, t]], jnp.float32)
                    is_own = c == core

                    @pl.when(is_own)
                    def _(t=t, b=b, j=j, row=row):
                        tab[c, t, b, j : j + 1] = row

                    @pl.when(jnp.logical_not(is_own))
                    def _(t=t, b=b, j=j, row=row):
                        tab_out[t, b, j : j + 1] = row
    tab_copy().start()
    live = []
    for t in range(slots):
        limit = jnp.where(mask_ref[0, t] == 1, len_ref[0] - order_ref[0, t] * tile, 0)
        place = lax.broadcasted_iota(jnp.int32, (tile, width), 0)
        live.append(jnp.where(place < limit, 1.0, 0.0).astype(jnp.bfloat16))
    for b in range(chips):
        other_values(b).wait()
        for t in range(slots):
            part = slice(t * tile, (t + 1) * tile)
            vals_out[b, part] = vals_out[b, part] * live[t]
        value_copy(b).start()
    for b in range(chips):
        own_values(b).wait()
        for t in range(slots):
            part = slice(t * tile, (t + 1) * tile)
            vals[b, c, part] = vals[b, c, part] * live[t]

    @pl.when(inner == 1)
    def _():
        for k in (2, 3):
            x_from(line[k]).wait_recv()
            x_forward(k).start()

    w_gather(0)
    score_scale = 0.5 / math.sqrt(head_dim)
    near = lax.div(z, 2)

    def half_at(b, core, side):
        return qs.at[b, core, pl.ds(side * 2, 2)]

    def q_out_at(side):
        return q_out.at[pl.ds(side * 2, 2)]

    def q_copy(side, k):
        piece = half_at(z, c, side)
        return remote(piece, piece, qsem.at[k], qr.at[z], line[k] * CORES + c)

    def q_cross(side, k):
        return remote(
            q_out_at(side), half_at(z, c, side), qf.at[k], qr.at[z], line[k] * CORES + (1 - c)
        )

    def query(side):
        block = xn[pl.ds(pl.multiple_of(side * pair, pair), pair)]
        half_query = 0.5 * jnp.dot(block, wq[0], preferred_element_type=jnp.float32)
        made = (silu_of_half(half_query) * score_scale).astype(jnp.bfloat16)
        parts = [
            made[:, core * width : (core + 1) * width].reshape(2, rows, width)
            for core in range(CORES)
        ]
        half_at(z, c, side)[...] = jnp.where(c == 0, parts[0], parts[1])
        q_out_at(side)[...] = jnp.where(c == 0, parts[1], parts[0])
        for k in reversed(range(1, chips)):
            q_copy(side, k).start()
            q_cross(side, k).start()
        q_cross(side, 0).start()

    @pl.when(inner == 1)
    def _():
        z_from(2).wait_recv()
        z_onward(2).start()

    for j in range(n_cand):
        w_across(0, j).wait_recv()
    x_from(line[1]).wait_recv()
    query(near)

    @pl.when(inner == 0)
    def _():
        for k in (2, 3):
            x_from(line[k]).wait_recv()

    query(1 - near)

    def g_copy(k):
        return remote(gate_out.at[line[k]], gate_in.at[z], gs.at[k], gr.at[z], line[k] * CORES + c)

    def g_from(k):
        slot = gate_in.at[line[k]]
        return remote(slot, slot, gs.at[k], gr.at[line[k]], sib)

    tab_from().wait_recv()
    for b in range(chips):
        own_keys(b).wait()
        key_from(b).wait_recv()
        value_from(b).wait_recv()

    def attend(b, side):
        query = qs[b, :, pl.ds(side * 2, 2)].reshape(CORES * 2 * rows, width)
        count = query.shape[0]
        lane = lax.broadcasted_iota(jnp.int32, (count, width), 1)
        in_head = [(lane >= j * head_dim) & (lane < (j + 1) * head_dim) for j in range(heads_here)]
        stack = jnp.concatenate(
            [query * jnp.where(at, 1.0, 0.0).astype(jnp.bfloat16) for at in in_head], axis=0
        )
        made = []
        for core in range(CORES):
            for t in range(slots):
                part = slice(t * tile, (t + 1) * tile)
                scores = lax.dot_general(
                    stack, keys[b, core, part], (((1,), (1,)), ((), ())),
                    preferred_element_type=jnp.float32,
                )
                bias = jnp.concatenate([tab[core, t, b]] * (tile // width), axis=1)
                half = jnp.concatenate(
                    [
                        scores[j * count : (j + 1) * count] + bias[j : j + 1]
                        for j in range(heads_here)
                    ],
                    axis=0,
                )
                made.append(silu_of_half(half).astype(jnp.bfloat16))
        total = jnp.dot(
            jnp.concatenate(made, axis=1), vals[b].reshape(CORES * events, width),
            preferred_element_type=jnp.float32,
        )
        result = total[:count]
        for j in range(1, heads_here):
            result = jnp.where(in_head[j], total[j * count : (j + 1) * count], result)
        return result.reshape(CORES, 2, rows, width).astype(jnp.bfloat16)

    def p_copy(b, zz, core):
        return remote(
            part_out.at[b, core, zz], part_in.at[h, b], ps.at[b], pr.at[h], zz * CORES + core
        )

    def step(k, carry):
        b = line_at(k)

        @pl.when(k == 0)
        def _():
            slot = qs.at[z, 1 - c]
            remote(slot, slot, qsem.at[0], qr.at[z], sib).wait_recv()

        @pl.when(k > 0)
        def _():
            remote(qs.at[b], qs.at[b], qsem.at[0], qr.at[b], sib).wait_recv()

        for side, group in ((1 - near, (3, 2)), (near, (1, 0))):
            part_out[b, :, pl.ds(side * 2, 2)] = attend(b, side)
            for i in group:
                if i > 0:
                    for core in range(CORES):
                        p_copy(b, line[i], core).start()
                else:
                    p_copy(b, z, 1 - c).start()
                    part_in[h, b] = part_out[b, c, z]

        @pl.when(k == 0)
        def _():
            w_gather(1)
            for j in range(n_cand):
                w_across(1, j).wait_recv()
            gate_out[...] = (
                silu_of_half(0.5 * jnp.dot(xn[...], wq[1], preferred_element_type=jnp.float32))
                .astype(jnp.bfloat16)
                .reshape(chips, rows, CORES * width)
            )
            for i in reversed(range(1, chips)):
                g_copy(i).start()
            gate_in[z] = gate_out[z]

        @pl.when((k == 0) & (inner == 0))
        def _():
            z_from(2).wait_recv()
            for j in range(1, n_cand):
                o_copy(j, 2).start()

        @pl.when((k == 1) & (inner == 0))
        def _():
            z_from(3).wait_recv()
            for j in range(1, n_cand):
                o_copy(j, 3).start()

        return carry

    z_from(1).wait_recv()
    for j in range(1, n_cand):
        o_copy(j, 1).start()

    @pl.when(inner == 1)
    def _():
        for j in range(1, n_cand):
            o_copy(j, 2).start()

    @pl.when(inner == 1)
    def _():
        z_from(3).wait_recv()
        z_onward(3).start()
        for j in range(1, n_cand):
            o_copy(j, 3).start()

    lax.fori_loop(0, chips, step, 0)
    stage_in[3].wait()
    o_sib().start()
    for j in range(1, n_cand):
        for k in range(chips):
            o_copy(n_cand - j, k).wait_recv()
        c_copy(j).start()

    for k in range(1, chips):
        g_from(k).wait_recv()
    for i in range(1, n_hist):
        hh = lax.rem(h + i, n_hist)
        remote(part_in.at[hh], part_in.at[hh], ps.at[0], pr.at[hh], sib).wait_recv()
    columns = []
    gate_columns = []
    for hh in range(n_hist):
        b, core = hh // CORES, hh % CORES
        piece = part_in[core, b].astype(jnp.float32)
        for i in range(1, chips):
            piece = piece + part_in[i * CORES + core, b].astype(jnp.float32)
        columns.append(piece)
        gate_columns.append(gate_in[b, :, core * width : (core + 1) * width].astype(jnp.float32))
    attended = jnp.concatenate(columns, axis=1)
    gates = jnp.concatenate(gate_columns, axis=1)
    gated = (layer_norm(attended, out_gain_ref[...]) * gates).astype(jnp.bfloat16)
    sides = [
        jnp.concatenate(
            [gated[:, hh * width : (hh + 1) * width] for hh in range(side, n_hist, CORES)], axis=1
        )
        for side in range(CORES)
    ]
    wide = wo_ref.shape[1]
    o_sib().wait_recv()
    for j in range(1, n_cand):
        c_copy(j).wait_recv()
    for n in range(n_cand):
        part = slice(n * wide, (n + 1) * wide)
        total = inputs_ref[0, :, part].astype(jnp.float32)
        for side in range(CORES):
            total += jnp.dot(
                sides[side], wo[n, side].reshape(chips * width, wide),
                preferred_element_type=jnp.float32,
            )
        out_ref[0, :, part] = total.astype(jnp.bfloat16)
    tab_copy().wait_send()
    for k in range(chips):
        key_copy(k).wait_send()
        value_copy(k).wait_send()
        remote(q_out, q_out, qf.at[k], qr.at[z], sib).wait_send()
        for i in range(2):
            w_onward(i, k).wait_send()
        if k > 0:
            sent = qs.at[z, c]
            remote(sent, sent, qsem.at[k], qr.at[z], sib).wait_send()
            w_copy(0, k).wait_send()
            w_copy(1, k).wait_send()
            g_copy(k).wait_send()
    for k in (1, 2):
        z_copy(k).wait_send()
        x_copy(line[k]).wait_send()

    @pl.when(inner == 1)
    def _():
        for k in (2, 3):
            z_onward(k).wait_send()
            x_forward(k).wait_send()

    o_sib().wait_send()
    for j in range(1, n_cand):
        for k in range(chips):
            o_copy(j, k).wait_send()
        c_copy(j).wait_send()
    for k in range(chips):
        sent = part_in.at[pl.ds(0, n_hist - 1), 0]
        remote(sent, sent, ps.at[k], pr.at[0], sib).wait_send()


def fused_shards(
    n_cand, n_hist, inputs, in_gain, w_qu, out_gain, w_out, hist_keys, hist_values, pos_bias,
    lengths, tile_order, tile_mask,
):
    chips = n_hist // CORES
    rows, features = inputs.shape[1:]
    depth, width = w_qu.shape[1:]
    events = hist_keys.shape[1]
    slots = tile_order.shape[1]
    heads_here = width * pos_bias.shape[0] // features
    half, full = jnp.bfloat16, jnp.float32
    vmem = pl.BlockSpec(memory_space=pltpu.VMEM)
    hbm = pl.BlockSpec(memory_space=pltpu.HBM)
    dma = pltpu.SemaphoreType.DMA
    return pl.pallas_call(
        functools.partial(fused, n_cand, chips),
        out_shape=pltpu.VMEM(inputs.shape, half),
        in_specs=[hbm] * 11,
        out_specs=vmem,
        scratch_shapes=[
            pltpu.VMEM(inputs.shape, half),
            pltpu.VMEM((1, features), full),
            pltpu.VMEM((1, features), full),
            pltpu.SMEM(pos_bias.shape, full),
            pltpu.SMEM(lengths.shape, jnp.int32),
            pltpu.SMEM(tile_order.shape, jnp.int32),
            pltpu.SMEM(tile_mask.shape, jnp.int32),
            dma((9,)),
            pltpu.VMEM((chips * rows, features), half),
            pltpu.VMEM((2, depth * n_cand, CORES * width), half),
            pltpu.VMEM((n_cand, CORES, chips, width, w_out.shape[1]), half),
            pltpu.VMEM((chips, CORES, events, width), half),
            pltpu.VMEM((chips, CORES, events, width), half),
            pltpu.VMEM((chips, events, width), half),
            pltpu.VMEM((CORES, slots, chips, heads_here, width), full),
            pltpu.VMEM((slots, chips, heads_here, width), full),
            pltpu.VMEM((chips, CORES, chips, rows, width), half),
            pltpu.VMEM((chips, rows, width), half),
            pltpu.VMEM((chips, rows, CORES * width), half),
            pltpu.VMEM((chips, rows, CORES * width), half),
            pltpu.VMEM((chips, CORES, chips, rows, width), half),
            pltpu.VMEM((n_hist, chips, rows, width), half),
            dma((chips,)), dma((chips,)), dma((chips,)),
            dma((chips,)), dma((chips,)),
            dma((chips,)), dma((chips,)),
            dma((1,)), dma((1,)),
            dma((chips,)), dma((chips,)),
            dma((2, n_cand)), dma((2, n_cand)),
            dma((2, n_cand)), dma((2, n_cand)),
            dma((chips,)), dma((chips,)),
            dma((n_cand, chips)), dma((n_cand, chips)),
            dma((n_cand,)), dma((n_cand,)),
            dma((chips,)), dma((chips,)),
            dma((chips,)), dma((chips,)),
            dma((chips,)), dma((n_hist,)),
            dma((chips,)), dma((chips,)),
        ],
        compiler_params=pltpu.CompilerParams(
            collective_id=0, has_side_effects=True, vmem_limit_bytes=60 * 1024 * 1024
        ),
    )(
        inputs, in_gain[None], w_qu, out_gain[None], w_out, hist_keys, hist_values, pos_bias,
        lengths, tile_order, tile_mask,
    )


def solution(mesh):
    n_cand, n_hist = mesh.shape["cand"], mesh.shape["hist"]

    def local(*arrays):
        depth, width = arrays[2].shape[1:]
        head_dim = arrays[0].shape[2] // arrays[7].shape[0]
        fits = n_hist == 4 * CORES and width % 128 == 0 and width % head_dim == 0
        if fits and depth % 16 == 0 and arrays[0].shape[2] == width * n_hist:
            return fused_shards(n_cand, n_hist, *arrays)
        return shards(*arrays)

    placed = (
        P("cand", "hist", None),
        P(),
        P(None, "cand", "hist"),
        P(),
        P("hist", "cand"),
        P("cand", "hist", None),
        P("cand", "hist", None),
        P(),
        P("cand"),
        P("cand", "hist"),
        P("cand", "hist"),
    )
    return jax.shard_map(
        local, mesh=mesh, in_specs=placed, out_specs=P("cand", "hist", None), check_vma=False
    )
```

```python
import functools
import math

import jax
import jax.numpy as jnp
from jax import lax
from jax.experimental import pallas as pl
from jax.experimental.pallas import tpu as pltpu
from jax.sharding import PartitionSpec as P

EPS = 1e-05


def layer_norm(values, gain_vector):
    row_mean = jnp.mean(values, axis=-1, keepdims=True)
    square = jnp.mean(values * values, axis=-1, keepdims=True)
    return (values - row_mean) * lax.rsqrt(square - row_mean * row_mean + EPS) * gain_vector


def attention(all_queries, hist_keys, hist_values, pos_bias, lengths, tile_order, tile_mask):
    cands = all_queries.shape[1]
    width = all_queries.shape[2]
    heads = pos_bias.shape[0]
    tiles_all = pos_bias.shape[1]
    slots = tile_order.shape[1]
    tile = hist_keys.shape[1] // slots
    head_dim = width // heads
    score_scale = 1.0 / math.sqrt(head_dim)
    tile_numbers = jnp.arange(tiles_all, dtype=jnp.int32)
    offsets = jnp.arange(tile, dtype=jnp.int32)

    def one_user(user_items):
        user_query, key_block, value_block, slot_order, slot_mask, length = user_items
        query_heads = user_query.reshape(cands, heads, head_dim)
        one_hot = (slot_order[:, None] == tile_numbers[None, :]).astype(jnp.float32)
        slot_bias = jnp.dot(one_hot, pos_bias.T, precision=lax.Precision.HIGHEST)
        summed = jnp.zeros((cands, heads, head_dim), jnp.float32)
        for slot_index in range(slots):
            key_tile = key_block[slot_index * tile : (slot_index + 1) * tile].reshape(
                tile, heads, head_dim
            )
            value_tile = value_block[slot_index * tile : (slot_index + 1) * tile].reshape(
                tile, heads, head_dim
            )
            positions = slot_order[slot_index] * tile + offsets
            is_live = ((slot_mask[slot_index] == 1) & (positions < length)).astype(jnp.float32)
            bias_row = slot_bias[slot_index]

            def compute(
                key_tile=key_tile, value_tile=value_tile, is_live=is_live, bias_row=bias_row
            ):
                scores = jnp.einsum(
                    "chd,ehd->che", query_heads, key_tile, preferred_element_type=jnp.float32
                )
                scores = scores * score_scale + bias_row[None, :, None]
                weights = (jax.nn.silu(scores) * is_live[None, None, :]).astype(jnp.bfloat16)
                return jnp.einsum(
                    "che,ehd->chd", weights, value_tile, preferred_element_type=jnp.float32
                )

            summed = summed + compute()
        return summed.reshape(cands, width)

    return lax.map(one_user, (all_queries, hist_keys, hist_values, tile_order, tile_mask, lengths))


def shards(
    inputs,
    in_gain,
    w_qu,
    out_gain,
    w_out,
    hist_keys,
    hist_values,
    pos_bias,
    lengths,
    tile_order,
    tile_mask,
):
    w_full, out_rows = (
        lax.all_gather(w_qu, "cand", axis=1, tiled=True),
        lax.all_gather(w_out, "cand", axis=1, tiled=True),
    )
    normed = layer_norm(inputs.astype(jnp.float32), in_gain).astype(jnp.bfloat16)
    projected = jnp.einsum(
        "ucd,jdk->ucjk",
        normed,
        lax.all_gather(w_full, "hist", axis=2, tiled=True),
        preferred_element_type=jnp.float32,
    )
    queries = jax.nn.silu(projected[:, :, 0]).astype(jnp.bfloat16)
    gates = jax.nn.silu(projected[:, :, 1])
    all_queries = lax.all_gather(queries, "hist", axis=1, tiled=True)
    attended = attention(
        all_queries, hist_keys, hist_values, pos_bias, lengths, tile_order, tile_mask
    )
    own_rows = lax.psum_scatter(
        attended.astype(jnp.bfloat16), "hist", scatter_dimension=1, tiled=True
    ).astype(jnp.float32)
    gated = (layer_norm(own_rows, out_gain) * gates).astype(jnp.bfloat16)
    projected_out = jnp.einsum(
        "uck,kd->ucd",
        gated,
        lax.all_gather(out_rows, "hist", axis=0, tiled=True),
        preferred_element_type=jnp.float32,
    )
    return (inputs.astype(jnp.float32) + projected_out).astype(jnp.bfloat16)


MESH = pl.DeviceIdType.MESH
CORES = 2


def silu_of_half(half):
    return half + half * jnp.tanh(half)


def fused(
    n_cand, chips, inputs_hbm, in_gain_hbm, w_ref, out_gain_hbm, wo_ref, k_hbm, v_hbm, bias_hbm,
    len_hbm, order_hbm, mask_hbm, out_ref,
    inputs_ref, in_gain_ref, out_gain_ref, bias_ref, len_ref, order_ref, mask_ref, in_sem, xn,
    wq, wo, keys, vals, vals_out, tab, tab_out, qs, q_out, gate_out, gate_in, part_out, part_in,
    k_own, v_own, v_other, ks, kr, vs, vr, ts, tr, xs, xr, fs, fr, ws, wr, zs, zr, os, orr, cs, cr,
    gs, gr, qsem, qr, ps, pr, xf, qf,
):
    n_hist = chips * CORES
    u = lax.axis_index("cand")
    h = lax.axis_index("hist")
    z = lax.div(h, CORES)
    c = lax.rem(h, CORES)
    sib = z * CORES + (1 - c)
    rows = inputs_hbm.shape[1]
    width = w_ref.shape[2]
    depth = w_ref.shape[1]
    features = inputs_hbm.shape[2]
    slots = order_ref.shape[1]
    events = k_hbm.shape[1]
    tile = events // slots
    pair = CORES * rows
    heads_here = width * bias_ref.shape[0] // features
    head_dim = width // heads_here

    inner = lax.rem(lax.div(z + 1, 2), 2)
    across = lax.rem(z + 2, chips)
    mirror = chips - 1 - z
    line = [
        z,
        z + 1 - 2 * lax.rem(z, 2),
        inner * mirror + (1 - inner) * across,
        inner * across + (1 - inner) * mirror,
    ]

    def line_at(k):
        place = line[chips - 1]
        for i in range(chips - 1):
            place = jnp.where(k == i, line[i], place)
        return place

    def chip_at(k):
        return lax.rem(z + k, chips)

    def remote(src, dst, send, recv, hist_to, cand_to=None):
        return pltpu.make_async_remote_copy(
            src_ref=src, dst_ref=dst, send_sem=send, recv_sem=recv,
            device_id=(u if cand_to is None else cand_to, hist_to), device_id_type=MESH,
        )

    mine = pl.ds(pl.multiple_of(c * width, width), width)
    theirs = pl.ds(pl.multiple_of((1 - c) * width, width), width)
    stage_in = [
        pltpu.make_async_copy(src, dst, in_sem.at[i])
        for i, (src, dst) in enumerate(
            (
                (inputs_hbm, inputs_ref),
                (in_gain_hbm, in_gain_ref),
                (w_ref, wq.at[:, pl.ds(pl.multiple_of(u * depth, depth), depth), mine]),
                (wo_ref, wo.at[u, c, z]),
                (out_gain_hbm, out_gain_ref),
                (bias_hbm, bias_ref),
                (len_hbm, len_ref),
                (order_hbm, order_ref),
                (mask_hbm, mask_ref),
            )
        )
    ]
    stage_in[0].start()
    stage_in[1].start()
    barrier = pltpu.get_barrier_semaphore()
    for i in range(1, n_hist):
        pl.semaphore_signal(
            barrier, inc=1, device_id=(u, lax.rem(h + i, n_hist)), device_id_type=MESH
        )
    for j in range(1, n_cand):
        pl.semaphore_signal(
            barrier, inc=1, device_id=(lax.rem(u + j, n_cand), h), device_id_type=MESH
        )
    for copy in stage_in[2:]:
        copy.start()

    def columns_of(ref, b, core):
        return ref.at[0, :, pl.ds(pl.multiple_of((b * CORES + core) * width, width), width)]

    def own_keys(b):
        return pltpu.make_async_copy(columns_of(k_hbm, b, c), keys.at[b, c], k_own.at[b])

    def own_values(b):
        return pltpu.make_async_copy(columns_of(v_hbm, b, c), vals.at[b, c], v_own.at[b])

    def other_values(b):
        return pltpu.make_async_copy(columns_of(v_hbm, b, 1 - c), vals_out.at[b], v_other.at[b])

    for b in range(chips):
        other_values(b).start()
    for b in range(chips):
        own_values(b).start()
        own_keys(b).start()

    stage_in[0].wait()
    stage_in[1].wait()
    normed = layer_norm(inputs_ref[0].astype(jnp.float32), in_gain_ref[...])

    def x_at(zz):
        return xn.at[pl.ds(pl.multiple_of(zz * rows, rows), rows)]

    x_at(z)[...] = normed.astype(jnp.bfloat16)
    pl.semaphore_wait(barrier, n_hist - 1 + n_cand - 1)

    def w_slot(i, uu):
        return wq.at[i, pl.ds(pl.multiple_of(uu * depth, depth), depth), mine]

    def w_copy(i, j):
        return remote(
            w_ref.at[i], w_slot(i, u), ws.at[i, j], wr.at[i, n_cand - j], h, lax.rem(u + j, n_cand)
        )

    def w_onward(i, j):
        slot = w_slot(i, lax.rem(u + j, n_cand))
        return remote(slot, slot, fs.at[i, j], fr.at[i, j], sib)

    def w_across(i, j):
        uu = lax.rem(u + j, n_cand)
        slot = wq.at[i, pl.ds(pl.multiple_of(uu * depth, depth), depth), theirs]
        return remote(slot, slot, fs.at[i, j], fr.at[i, j], sib)

    def w_gather(i):
        for j in range(1, n_cand):
            w_copy(i, n_cand - j).wait_recv()
            w_onward(i, j).start()

    def z_copy(k):
        return remote(wo_ref, wo.at[u, c, z], zs.at[k], zr.at[z], line[k] * CORES + c)

    def z_from(k):
        slot = wo.at[u, c, line[k]]
        return remote(slot, slot, zs.at[k], zr.at[line[k]], sib)

    def z_onward(k):
        slot = wo.at[u, c, line[k]]
        return remote(slot, slot, zs.at[3 * (k - 2)], zr.at[line[k]], line[1] * CORES + c)

    def o_sib():
        return remote(wo.at[u, c], wo.at[u, c], os.at[0, 0], orr.at[0, 0], sib)

    def o_copy(j, k):
        slot = wo.at[u, c, line[k]]
        return remote(
            wo_ref if k == 0 else slot, slot, os.at[j, k], orr.at[n_cand - j, k], h,
            lax.rem(u + j, n_cand),
        )

    def c_copy(j):
        uu = lax.rem(u + j, n_cand)
        return remote(wo.at[uu, c], wo.at[uu, c], cs.at[j], cr.at[j], sib)

    def x_copy(zz):
        return remote(x_at(z), x_at(z), xs.at[zz], xr.at[z], zz * CORES + c)

    def x_from(zz):
        return remote(x_at(zz), x_at(zz), xs.at[zz], xr.at[zz], sib)

    def x_forward(k):
        return remote(
            x_at(line[k]), x_at(line[k]), xf.at[k], xr.at[line[k]], line[1] * CORES + c
        )

    def key_copy(b):
        return remote(columns_of(k_hbm, b, 1 - c), keys.at[b, c], ks.at[b], kr.at[b], sib)

    def value_copy(b):
        return remote(vals_out.at[b], vals.at[b, c], vs.at[b], vr.at[b], sib)

    def key_from(b):
        return remote(keys.at[b, 1 - c], keys.at[b, 1 - c], ks.at[b], kr.at[b], sib)

    def value_from(b):
        return remote(vals.at[b, 1 - c], vals.at[b, 1 - c], vs.at[b], vr.at[b], sib)

    def tab_copy():
        return remote(tab_out, tab.at[c], ts.at[0], tr.at[0], sib)

    def tab_from():
        return remote(tab_out, tab.at[1 - c], ts.at[0], tr.at[0], sib)

    for j in range(1, n_cand):
        w_copy(0, j).start()
    for k in (2, 1):
        x_copy(line[k]).start()
    z_copy(1).start()
    z_copy(2).start()
    for j in range(1, n_cand):
        o_copy(j, 0).start()
    for j in range(1, n_cand):
        w_copy(1, j).start()
    stage_in[2].wait()
    w_onward(0, 0).start()
    w_onward(1, 0).start()
    for b in range(chips):
        key_copy(b).start()

    for copy in stage_in[4:]:
        copy.wait()
    for t in range(slots):
        for b in range(chips):
            for j in range(heads_here):
                for core in range(CORES):
                    head = (b * CORES + core) * heads_here + j
                    row = jnp.full((1, width), 0.5 * bias_ref[head, order_ref[0, t]], jnp.float32)
                    is_own = c == core

                    @pl.when(is_own)
                    def _(t=t, b=b, j=j, row=row):
                        tab[c, t, b, j : j + 1] = row

                    @pl.when(jnp.logical_not(is_own))
                    def _(t=t, b=b, j=j, row=row):
                        tab_out[t, b, j : j + 1] = row
    tab_copy().start()
    live = []
    for t in range(slots):
        limit = jnp.where(mask_ref[0, t] == 1, len_ref[0] - order_ref[0, t] * tile, 0)
        place = lax.broadcasted_iota(jnp.int32, (tile, width), 0)
        live.append(jnp.where(place < limit, 1.0, 0.0).astype(jnp.bfloat16))
    for b in range(chips):
        other_values(b).wait()
        for t in range(slots):
            part = slice(t * tile, (t + 1) * tile)
            vals_out[b, part] = vals_out[b, part] * live[t]
        value_copy(b).start()
    for b in range(chips):
        own_values(b).wait()
        for t in range(slots):
            part = slice(t * tile, (t + 1) * tile)
            vals[b, c, part] = vals[b, c, part] * live[t]

    @pl.when(inner == 1)
    def _():
        for k in (2, 3):
            x_from(line[k]).wait_recv()
            x_forward(k).start()

    w_gather(0)
    score_scale = 0.5 / math.sqrt(head_dim)
    near = lax.div(z, 2)

    def half_at(b, core, side):
        return qs.at[b, core, pl.ds(side * 2, 2)]

    def q_out_at(side):
        return q_out.at[pl.ds(side * 2, 2)]

    def q_copy(side, k):
        piece = half_at(z, c, side)
        return remote(piece, piece, qsem.at[k], qr.at[z], line[k] * CORES + c)

    def q_cross(side, k):
        return remote(
            q_out_at(side), half_at(z, c, side), qf.at[k], qr.at[z], line[k] * CORES + (1 - c)
        )

    def query(side):
        block = xn[pl.ds(pl.multiple_of(side * pair, pair), pair)]
        half_query = 0.5 * jnp.dot(block, wq[0], preferred_element_type=jnp.float32)
        made = (silu_of_half(half_query) * score_scale).astype(jnp.bfloat16)
        parts = [
            made[:, core * width : (core + 1) * width].reshape(2, rows, width)
            for core in range(CORES)
        ]
        half_at(z, c, side)[...] = jnp.where(c == 0, parts[0], parts[1])
        q_out_at(side)[...] = jnp.where(c == 0, parts[1], parts[0])
        for k in reversed(range(1, chips)):
            q_copy(side, k).start()
            q_cross(side, k).start()
        q_cross(side, 0).start()

    @pl.when(inner == 1)
    def _():
        z_from(2).wait_recv()
        z_onward(2).start()

    for j in range(n_cand):
        w_across(0, j).wait_recv()
    x_from(line[1]).wait_recv()
    query(near)

    @pl.when(inner == 0)
    def _():
        for k in (2, 3):
            x_from(line[k]).wait_recv()

    query(1 - near)

    def g_copy(k):
        return remote(gate_out.at[line[k]], gate_in.at[z], gs.at[k], gr.at[z], line[k] * CORES + c)

    def g_from(k):
        slot = gate_in.at[line[k]]
        return remote(slot, slot, gs.at[k], gr.at[line[k]], sib)


    def attend(b, side):
        query = qs[b, :, pl.ds(side * 2, 2)].reshape(CORES * 2 * rows, width)
        count = query.shape[0]
        lane = lax.broadcasted_iota(jnp.int32, (count, width), 1)
        in_head = [(lane >= j * head_dim) & (lane < (j + 1) * head_dim) for j in range(heads_here)]
        stack = jnp.concatenate(
            [query * jnp.where(at, 1.0, 0.0).astype(jnp.bfloat16) for at in in_head], axis=0
        )
        made = []
        for core in range(CORES):
            for t in range(slots):
                part = slice(t * tile, (t + 1) * tile)
                scores = lax.dot_general(
                    stack, keys[b, core, part], (((1,), (1,)), ((), ())),
                    preferred_element_type=jnp.float32,
                )
                bias = jnp.concatenate([tab[core, t, b]] * (tile // width), axis=1)
                half = jnp.concatenate(
                    [
                        scores[j * count : (j + 1) * count] + bias[j : j + 1]
                        for j in range(heads_here)
                    ],
                    axis=0,
                )
                made.append(silu_of_half(half).astype(jnp.bfloat16))
        total = jnp.dot(
            jnp.concatenate(made, axis=1), vals[b].reshape(CORES * events, width),
            preferred_element_type=jnp.float32,
        )
        result = total[:count]
        for j in range(1, heads_here):
            result = jnp.where(in_head[j], total[j * count : (j + 1) * count], result)
        return result.reshape(CORES, 2, rows, width).astype(jnp.bfloat16)

    def p_copy(b, zz, core):
        return remote(
            part_out.at[b, core, zz], part_in.at[h, b], ps.at[b], pr.at[h], zz * CORES + core
        )

    def step(k, carry):
        b = line_at(k)

        @pl.when(k == 0)
        def _():
            slot = qs.at[z, 1 - c]
            remote(slot, slot, qsem.at[0], qr.at[z], sib).wait_recv()

        @pl.when(k > 0)
        def _():
            remote(qs.at[b], qs.at[b], qsem.at[0], qr.at[b], sib).wait_recv()

        for side, group in ((1 - near, (3, 2)), (near, (1, 0))):
            part_out[b, :, pl.ds(side * 2, 2)] = attend(b, side)
            for i in group:
                if i > 0:
                    for core in reversed(range(CORES)):
                        p_copy(b, line[i], core).start()
                else:
                    p_copy(b, z, 1 - c).start()
                    part_in[h, b] = part_out[b, c, z]

        @pl.when(k == 0)
        def _():
            for j in range(n_cand):
                w_across(1, j).wait_recv()
            gate_out[...] = (
                silu_of_half(0.5 * jnp.dot(xn[...], wq[1], preferred_element_type=jnp.float32))
                .astype(jnp.bfloat16)
                .reshape(chips, rows, CORES * width)
            )
            for i in reversed(range(1, chips)):
                g_copy(i).start()
            gate_in[z] = gate_out[z]

        @pl.when((k == 0) & (inner == 0))
        def _():
            z_from(2).wait_recv()
            for j in range(1, n_cand):
                o_copy(j, 2).start()

        @pl.when((k == 1) & (inner == 0))
        def _():
            z_from(3).wait_recv()
            for j in range(1, n_cand):
                o_copy(j, 3).start()

        return carry

    @pl.when(inner == 1)
    def _():
        z_from(3).wait_recv()
        z_onward(3).start()

    z_from(1).wait_recv()
    for j in range(1, n_cand):
        o_copy(j, 1).start()

    @pl.when(inner == 1)
    def _():
        for k in (2, 3):
            for j in range(1, n_cand):
                o_copy(j, k).start()

    w_gather(1)
    tab_from().wait_recv()
    for b in range(chips):
        own_keys(b).wait()
        key_from(b).wait_recv()
        value_from(b).wait_recv()
    lax.fori_loop(0, chips, step, 0)
    stage_in[3].wait()
    o_sib().start()
    for j in range(1, n_cand):
        for k in range(chips):
            o_copy(n_cand - j, k).wait_recv()
        c_copy(j).start()

    for k in range(1, chips):
        g_from(k).wait_recv()
    for i in range(1, n_hist):
        hh = lax.rem(h + i, n_hist)
        remote(part_in.at[hh], part_in.at[hh], ps.at[0], pr.at[hh], sib).wait_recv()
    columns = []
    gate_columns = []
    for hh in range(n_hist):
        b, core = hh // CORES, hh % CORES
        piece = part_in[core, b].astype(jnp.float32)
        for i in range(1, chips):
            piece = piece + part_in[i * CORES + core, b].astype(jnp.float32)
        columns.append(piece)
        gate_columns.append(gate_in[b, :, core * width : (core + 1) * width].astype(jnp.float32))
    attended = jnp.concatenate(columns, axis=1)
    gates = jnp.concatenate(gate_columns, axis=1)
    gated = (layer_norm(attended, out_gain_ref[...]) * gates).astype(jnp.bfloat16)
    sides = [
        jnp.concatenate(
            [gated[:, hh * width : (hh + 1) * width] for hh in range(side, n_hist, CORES)], axis=1
        )
        for side in range(CORES)
    ]
    wide = wo_ref.shape[1]
    o_sib().wait_recv()
    for j in range(1, n_cand):
        c_copy(j).wait_recv()
    for n in range(n_cand):
        part = slice(n * wide, (n + 1) * wide)
        total = inputs_ref[0, :, part].astype(jnp.float32)
        for side in range(CORES):
            total += jnp.dot(
                sides[side], wo[n, side].reshape(chips * width, wide),
                preferred_element_type=jnp.float32,
            )
        out_ref[0, :, part] = total.astype(jnp.bfloat16)
    tab_copy().wait_send()
    for k in range(chips):
        key_copy(k).wait_send()
        value_copy(k).wait_send()
        remote(q_out, q_out, qf.at[k], qr.at[z], sib).wait_send()
        for i in range(2):
            w_onward(i, k).wait_send()
        if k > 0:
            sent = qs.at[z, c]
            remote(sent, sent, qsem.at[k], qr.at[z], sib).wait_send()
            w_copy(0, k).wait_send()
            w_copy(1, k).wait_send()
            g_copy(k).wait_send()
    for k in (1, 2):
        z_copy(k).wait_send()
        x_copy(line[k]).wait_send()

    @pl.when(inner == 1)
    def _():
        for k in (2, 3):
            z_onward(k).wait_send()
            x_forward(k).wait_send()

    o_sib().wait_send()
    for j in range(1, n_cand):
        for k in range(chips):
            o_copy(j, k).wait_send()
        c_copy(j).wait_send()
    for k in range(chips):
        sent = part_in.at[pl.ds(0, n_hist - 1), 0]
        remote(sent, sent, ps.at[k], pr.at[0], sib).wait_send()


def fused_shards(
    n_cand, n_hist, inputs, in_gain, w_qu, out_gain, w_out, hist_keys, hist_values, pos_bias,
    lengths, tile_order, tile_mask,
):
    chips = n_hist // CORES
    rows, features = inputs.shape[1:]
    depth, width = w_qu.shape[1:]
    events = hist_keys.shape[1]
    slots = tile_order.shape[1]
    heads_here = width * pos_bias.shape[0] // features
    half, full = jnp.bfloat16, jnp.float32
    vmem = pl.BlockSpec(memory_space=pltpu.VMEM)
    hbm = pl.BlockSpec(memory_space=pltpu.HBM)
    dma = pltpu.SemaphoreType.DMA
    return pl.pallas_call(
        functools.partial(fused, n_cand, chips),
        out_shape=pltpu.VMEM(inputs.shape, half),
        in_specs=[hbm] * 11,
        out_specs=vmem,
        scratch_shapes=[
            pltpu.VMEM(inputs.shape, half),
            pltpu.VMEM((1, features), full),
            pltpu.VMEM((1, features), full),
            pltpu.SMEM(pos_bias.shape, full),
            pltpu.SMEM(lengths.shape, jnp.int32),
            pltpu.SMEM(tile_order.shape, jnp.int32),
            pltpu.SMEM(tile_mask.shape, jnp.int32),
            dma((9,)),
            pltpu.VMEM((chips * rows, features), half),
            pltpu.VMEM((2, depth * n_cand, CORES * width), half),
            pltpu.VMEM((n_cand, CORES, chips, width, w_out.shape[1]), half),
            pltpu.VMEM((chips, CORES, events, width), half),
            pltpu.VMEM((chips, CORES, events, width), half),
            pltpu.VMEM((chips, events, width), half),
            pltpu.VMEM((CORES, slots, chips, heads_here, width), full),
            pltpu.VMEM((slots, chips, heads_here, width), full),
            pltpu.VMEM((chips, CORES, chips, rows, width), half),
            pltpu.VMEM((chips, rows, width), half),
            pltpu.VMEM((chips, rows, CORES * width), half),
            pltpu.VMEM((chips, rows, CORES * width), half),
            pltpu.VMEM((chips, CORES, chips, rows, width), half),
            pltpu.VMEM((n_hist, chips, rows, width), half),
            dma((chips,)), dma((chips,)), dma((chips,)),
            dma((chips,)), dma((chips,)),
            dma((chips,)), dma((chips,)),
            dma((1,)), dma((1,)),
            dma((chips,)), dma((chips,)),
            dma((2, n_cand)), dma((2, n_cand)),
            dma((2, n_cand)), dma((2, n_cand)),
            dma((chips,)), dma((chips,)),
            dma((n_cand, chips)), dma((n_cand, chips)),
            dma((n_cand,)), dma((n_cand,)),
            dma((chips,)), dma((chips,)),
            dma((chips,)), dma((chips,)),
            dma((chips,)), dma((n_hist,)),
            dma((chips,)), dma((chips,)),
        ],
        compiler_params=pltpu.CompilerParams(
            collective_id=0, has_side_effects=True, vmem_limit_bytes=60 * 1024 * 1024
        ),
    )(
        inputs, in_gain[None], w_qu, out_gain[None], w_out, hist_keys, hist_values, pos_bias,
        lengths, tile_order, tile_mask,
    )


def solution(mesh):
    n_cand, n_hist = mesh.shape["cand"], mesh.shape["hist"]

    def local(*arrays):
        depth, width = arrays[2].shape[1:]
        head_dim = arrays[0].shape[2] // arrays[7].shape[0]
        fits = n_hist == 4 * CORES and width % 128 == 0 and width % head_dim == 0
        if fits and depth % 16 == 0 and arrays[0].shape[2] == width * n_hist:
            return fused_shards(n_cand, n_hist, *arrays)
        return shards(*arrays)

    placed = (
        P("cand", "hist", None),
        P(),
        P(None, "cand", "hist"),
        P(),
        P("hist", "cand"),
        P("cand", "hist", None),
        P("cand", "hist", None),
        P(),
        P("cand"),
        P("cand", "hist"),
        P("cand", "hist"),
    )
    return jax.shard_map(
        local, mesh=mesh, in_specs=placed, out_specs=P("cand", "hist", None), check_vma=False
    )
```
